256 devices in a mesh: star: 8 (over x, core), row: 32 (over z, y).
Axes of the slice: x: 4, y: 4, z: 8, core: 2. Of those that a mesh axis runs over, the one named last changes fastest.
Arguments:
- feature_maps: bfloat16 [64, 1024, 1024], P(None, 'row'), may hold values from -6 to 6
- coef_table: bfloat16 [64, 64], replicated, may hold values from -0.119628906 to 0.119628906
- star_counts: int32 [8], replicated, may hold values from 1 to 12, 32 in all
- star_cells: int32 [8, 12], replicated, may hold values from 0 to 63
- star_bands: int32 [8, 12], replicated, may hold values from 0 to 7
- psf_cotangent: bfloat16 [96, 1024, 1024], P('star', 'row'), may hold values from -6 to 6
Outputs:
- map_grad: float32 [64, 1024, 1024], P('star', 'row')
- coef_grad: float32 [64, 64], replicated
The draws below stay inside these ranges and needn't reach their ends.
Inputs may be any that keep to these rules, and one draw needn't show every extreme that they name: The live stars of group g fill its slots 0 to star_counts[g] - 1; the counts sum to 32, and some group has exactly 12.
All inputs are finite; a program needn't handle non-finite values.
Results may differ from the reference program's by a relative error of at most 0.008.
Values may be sent and summed in bfloat16 or wider, within the bound.
No kernel may reach another device: no remote copies, remote signals or barrier semaphores. Data moves between devices by JAX's collectives and lax.ppermute only.
A program may use at most 128 MiB of HBM per device.

```python
import math
import jax
import jax.numpy as jnp
import numpy as np
from jax import lax

PUPIL = 1024
MAPS = 64
CELLS = 64
BANDS = 8
SLOT = 12
TOTAL = 32
N_STAR = 8


def spread_values(key, limit, length):
    first_key, second_key = jax.random.split(key)
    values = jax.random.randint(first_key, (length,), 0, limit, dtype=jnp.int32)
    places = jax.random.permutation(second_key, length)
    values = values.at[places[0]].set(limit - 1)
    return values.at[places[1]].set(0)


def draw_star_cells(key, part):
    return spread_values(jax.random.fold_in(key, 11), CELLS, N_STAR * SLOT).reshape(N_STAR, SLOT)


def draw_star_bands(key, part):
    return spread_values(jax.random.fold_in(key, 23), BANDS, N_STAR * SLOT).reshape(N_STAR, SLOT)


def steps_of(stream_key, extent, shards, smallest, largest):
    def one(axis_at, blocks):
        draws = jax.random.uniform(jax.random.fold_in(jax.random.fold_in(stream_key, 6), axis_at), (blocks,), jnp.float32, smallest / len(shards), largest / len(shards))
        return jnp.repeat(jnp.exp(draws), extent[axis_at] // blocks).reshape((-1,) + (1,) * (len(extent) - axis_at - 1))

    factor_of = one(*shards[0])
    for cut in shards[1:]:
        factor_of = factor_of * one(*cut)
    return factor_of


def split_up(number_of, total, most, lean):
    loads = [(1 << 20) // math.isqrt(rank ** lean) + 1 for rank in range(2, number_of + 1)]
    spare, holding = total - most - (number_of - 1), [1] * (number_of - 1)
    while spare > 0:
        free = [i for i in range(number_of - 1) if holding[i] < most]
        mass, budget = sum([loads[i] for i in free]), spare
        for i in free:
            more = min(most - holding[i], max(1, budget * loads[i] // mass), spare)
            holding[i] = holding[i] + more
            spare = spare - more
    return np.array([most] + holding)


def uneven_parts(rng, number_of, total, bound, slope):
    if number_of == 2:
        one = jax.random.randint(rng, (), max(1, total - bound), min(bound, total - 1) + 1)
        return jnp.stack([one, total - one])
    sizes = jnp.asarray(split_up(number_of, total, bound, slope), jnp.int32)
    twos = (number_of - 1) // 2
    donor, sink = sizes[1:1 + 2 * twos:2], sizes[2:2 + 2 * twos:2]
    slack = jnp.minimum(donor - 1, bound - sink)
    passed = jax.random.randint(jax.random.fold_in(rng, 1), (twos,), 0, 1 << 20) % (slack + 1)
    sizes = sizes.at[1:1 + 2 * twos:2].set(donor - passed).at[2:2 + 2 * twos:2].set(sink + passed)
    return sizes[jax.random.permutation(jax.random.fold_in(rng, 2), number_of)]


def noise(key, extent, scale, bound, shards=(), kind=jnp.bfloat16):
    level = steps_of(key, extent, shards, -0.22, 0.18) if shards else 1.0
    result = jax.random.normal(key, extent, jnp.float32) * scale * level
    return jnp.minimum(jnp.maximum(result, -bound), bound).astype(kind)


def setup_inputs(seed: int = 0) -> dict:
    key_of = jax.random.split(jax.random.key(seed), 7)
    feature_maps = noise(key_of[0], (MAPS, PUPIL, PUPIL), 1.0, 6.0, ((1, 32),))
    coef_table = noise(key_of[1], (CELLS, MAPS), 0.02, 0.119628906)
    star_counts = uneven_parts(key_of[2], N_STAR, TOTAL, SLOT, 2).astype(jnp.int32)
    star_cells = draw_star_cells(jax.random.fold_in(key_of[6], 71), 0)
    star_bands = draw_star_bands(jax.random.fold_in(key_of[6], 71), 0)
    psf_cotangent = noise(key_of[5], (N_STAR * SLOT, PUPIL, PUPIL), 1.0, 6.0, ((0, 8), (1, 32)))
    return {"feature_maps": feature_maps, "coef_table": coef_table, "star_counts": star_counts, "star_cells": star_cells, "star_bands": star_bands, "psf_cotangent": psf_cotangent}


def fourier_tables(pupil_size):
    index_row = jnp.arange(pupil_size, dtype=jnp.int32)
    products = (index_row[:, None] * index_row[None, :]) % pupil_size
    angles = (2.0 * jnp.pi / pupil_size) * products.astype(jnp.float32)
    return jnp.cos(angles).astype(jnp.bfloat16), (-jnp.sin(angles)).astype(jnp.bfloat16)


def aperture_rows(first_row, row_count, pupil_size):
    centre = 0.5 * (pupil_size - 1)
    row_pos = (first_row + jnp.arange(row_count, dtype=jnp.int32)).astype(jnp.float32) - centre
    col_pos = jnp.arange(pupil_size, dtype=jnp.int32).astype(jnp.float32) - centre
    radius = row_pos[:, None] * row_pos[:, None] + col_pos[None, :] * col_pos[None, :]
    return jnp.where(radius <= 0.25 * pupil_size * pupil_size, 1.0, 0.0).astype(jnp.float32)


def wave_numbers(band_ids):
    wavelength = 0.55 + 0.35 * band_ids.astype(jnp.float32) / (BANDS - 1)
    return 2.0 * jnp.pi / wavelength


def product(left, right):
    return jnp.dot(left.astype(jnp.float32), right.astype(jnp.float32), precision=lax.Precision.HIGHEST)


def star_gradient(flat_maps, coef_row, band_id, cotangent, cos_table, sin_table, aperture):
    pupil_size = aperture.shape[0]
    path_error = product(coef_row[None, :], flat_maps)[0].reshape(pupil_size, pupil_size)
    wave_number = wave_numbers(band_id)
    phase_angle = wave_number * path_error
    cos_phase = jnp.cos(phase_angle)
    sin_phase = jnp.sin(phase_angle)
    pupil_real = (aperture * cos_phase).astype(jnp.bfloat16)
    pupil_imag = (aperture * sin_phase).astype(jnp.bfloat16)
    column_real = (product(pupil_real, cos_table) - product(pupil_imag, sin_table)).astype(jnp.bfloat16)
    column_imag = (product(pupil_real, sin_table) + product(pupil_imag, cos_table)).astype(jnp.bfloat16)
    inverse = 1.0 / pupil_size
    focal_real = (product(column_real.T, cos_table) - product(column_imag.T, sin_table)) * inverse
    focal_imag = (product(column_real.T, sin_table) + product(column_imag.T, cos_table)) * inverse
    grad_real = (2.0 * cotangent * focal_real).astype(jnp.bfloat16)
    grad_imag = (2.0 * cotangent * focal_imag).astype(jnp.bfloat16)
    back_real = ((product(grad_real, cos_table) + product(grad_imag, sin_table)) * inverse).astype(jnp.bfloat16)
    back_imag = ((product(grad_imag, cos_table) - product(grad_real, sin_table)) * inverse).astype(jnp.bfloat16)
    pupil_greal = product(back_real.T, cos_table) + product(back_imag.T, sin_table)
    pupil_gimag = product(back_imag.T, cos_table) - product(back_real.T, sin_table)
    phase_grad = aperture * (cos_phase * pupil_gimag - sin_phase * pupil_greal)
    return (wave_number * phase_grad).astype(jnp.bfloat16)


def reference(feature_maps, coef_table, star_counts, star_cells, star_bands, psf_cotangent):
    map_count = feature_maps.shape[0]
    pupil_size = feature_maps.shape[1]
    slot_count = star_cells.shape[1]
    flat_maps = feature_maps.reshape(map_count, pupil_size * pupil_size).astype(jnp.float32)
    cos_table, sin_table = fourier_tables(pupil_size)
    aperture = aperture_rows(0, pupil_size, pupil_size)
    group_ends = jnp.cumsum(star_counts).astype(jnp.int32)
    group_starts = (group_ends - star_counts).astype(jnp.int32)
    flat_cells = star_cells.reshape(-1)
    flat_bands = star_bands.reshape(-1)

    def star_step(running, star_rank):
        map_total, coef_total = running
        owner_group = jnp.sum((group_ends <= star_rank).astype(jnp.int32)).astype(jnp.int32)
        slot_index = (owner_group * slot_count + star_rank - group_starts[owner_group]).astype(jnp.int32)
        cell_id = flat_cells[slot_index]
        band_id = flat_bands[slot_index]
        coef_row = coef_table[cell_id].astype(jnp.float32)
        cotangent = lax.dynamic_index_in_dim(psf_cotangent, slot_index, 0, keepdims=False).astype(jnp.float32)
        path_grad = star_gradient(flat_maps, coef_row, band_id, cotangent, cos_table, sin_table, aperture)
        flat_grad = path_grad.reshape(1, pupil_size * pupil_size).astype(jnp.float32)
        map_total = map_total + product(coef_row[:, None], flat_grad)
        map_scores = product(flat_maps, flat_grad.T)[:, 0] / (8 * pupil_size)
        coef_total = coef_total.at[cell_id].add(map_scores)
        return (map_total, coef_total), jnp.zeros((), jnp.float32)

    initial = (jnp.zeros((map_count, pupil_size * pupil_size), jnp.float32), jnp.zeros(coef_table.shape, jnp.float32))
    finished, unused = lax.scan(star_step, initial, jnp.arange(TOTAL, dtype=jnp.int32))
    return finished[0].reshape(map_count, pupil_size, pupil_size), finished[1]
```

```python
import jax
import jax.numpy as jnp
import numpy as np
from jax import lax
from jax.experimental import pallas as pl
from jax.experimental.pallas import tpu as pltpu
from jax.sharding import PartitionSpec as P

BF = jnp.bfloat16
F32 = jnp.float32
N = 1024
MAPS = 64
BLK = 32
GROUPS = 8
SLOT = 12
TOTAL = 32
MINE = 4
WAVES = [float(np.float32(2.0 * np.pi) / np.float32(0.55 + 0.35 * b / 7)) for b in range(8)]
TURNS = [float(1.0 / (0.55 + 0.35 * b / 7)) for b in range(8)]
VMEM_SPEC = pl.BlockSpec(memory_space=pltpu.VMEM)
SMEM_SPEC = pl.BlockSpec(memory_space=pltpu.SMEM)
ANY_SPEC = pl.BlockSpec(memory_space=pl.ANY)
NN = (((1,), (0,)), ((), ()))
NT = (((1,), (1,)), ((), ()))
TN = (((0,), (0,)), ((), ()))


def dot(a, b, dims=NN, precision=None):
    return lax.dot_general(a, b, dims, precision=precision, preferred_element_type=F32)


def iota(shape, axis):
    return lax.broadcasted_iota(jnp.int32, shape, axis)


def params(mib):
    return pltpu.CompilerParams(vmem_limit_bytes=mib << 20)


def table_seeds():
    b = np.arange(N, dtype=np.int64)
    low = (np.arange(32)[:, None] * b[None, :]) % N
    high = (32 * np.arange(32)[:, None] * b[None, :]) % N
    both = np.stack([low, high]) * (2.0 * np.pi / N)
    return np.stack([np.cos(both), -np.sin(both)], 1).astype(np.float32)


def fit_polynomials():
    x = 0.125 * (1.0 + np.cos(np.pi * (np.arange(4000) + 0.5) / 4000))
    f = np.sqrt(x)
    cheb = np.polynomial.chebyshev.Chebyshev
    poly = np.polynomial.polynomial.Polynomial
    c = cheb.fit(x, np.cos(2 * np.pi * f), 8, domain=[0, 0.25]).convert(kind=poly)
    s = cheb.fit(x, np.sin(2 * np.pi * f) / f, 8, domain=[0, 0.25]).convert(kind=poly)
    return [float(v) for v in c.coef], [float(v) for v in s.coef]


COS_POLY, SIN_POLY = fit_polynomials()


def cos_sin_turns(f):
    x = f * f
    c = jnp.full_like(f, COS_POLY[-1])
    s = jnp.full_like(f, SIN_POLY[-1])
    for k in range(len(COS_POLY) - 2, -1, -1):
        c = c * x + COS_POLY[k]
        s = s * x + SIN_POLY[k]
    return c, s * f


def my_bands(counts_ref, bands_ref, group):
    starts, total = [], jnp.int32(0)
    for g in range(GROUPS):
        starts.append(total)
        total = total + counts_ref[g]
    out = []
    for j in range(MINE):
        q = group * MINE + j
        owner, first = jnp.int32(0), jnp.int32(0)
        for g in range(1, GROUPS):
            here = q >= starts[g]
            owner = jnp.where(here, g, owner)
            first = jnp.where(here, starts[g], first)
        out.append(bands_ref[owner, q - first])
    return out


def pick(values, index):
    chosen = jnp.float32(values[0])
    for k in range(1, len(values)):
        chosen = jnp.where(index == k, jnp.float32(values[k]), chosen)
    return chosen


def aperture_mask(first_row, rows):
    centre = 0.5 * (N - 1)
    y = (first_row + iota((rows, N), 0)).astype(F32) - centre
    x = iota((rows, N), 1).astype(F32) - centre
    return y * y + x * x <= 0.25 * N * N


def pack_kernel(counts_ref, cells_ref, table_ref, psf_ref, packed_ref, coef_ref, hot_ref, held, in_sem, out_sem):
    me = lax.axis_index("star")
    load = pltpu.make_async_copy(psf_ref, held.at[pl.ds(0, SLOT)], in_sem)
    load.start()
    held[SLOT] = jnp.zeros((BLK, N), BF)
    row32 = iota((TOTAL, MAPS), 0)
    row64 = iota((2 * TOTAL, MAPS), 0)
    cell32 = jnp.full((TOTAL, MAPS), -1, jnp.int32)
    cell64 = jnp.full((2 * TOTAL, MAPS), -1, jnp.int32)
    total = jnp.int32(0)
    start = jnp.int32(0)
    for g in range(GROUPS):
        count = counts_ref[g]
        start = jnp.where(me == g, total, start)
        for j in range(SLOT):
            q = jnp.where(j < count, total + j, -1)
            cell = cells_ref[g, j]
            q64 = jnp.where(q < 0, -1, 2 * q - q % MINE)
            cell32 = jnp.where(row32 == q, cell, cell32)
            cell64 = jnp.where(row64 == q64, cell, cell64)
        total = total + count
    mine = counts_ref[me]
    hot32 = jnp.where(iota((TOTAL, MAPS), 1) == cell32, 1.0, 0.0).astype(BF)
    coef_ref[...] = dot(hot32, table_ref[...]).astype(BF)
    hot_ref[...] = jnp.where(iota((2 * TOTAL, MAPS), 1) == cell64, 1.0, 0.0)
    load.wait()
    copies = []
    for q in range(TOTAL):
        j = q - start
        source = jnp.where((j >= 0) & (j < mine), j, SLOT)
        copy = pltpu.make_async_copy(held.at[source], packed_ref.at[q], out_sem.at[q])
        copy.start()
        copies.append(copy)
    for copy in copies:
        copy.wait()


def pack(counts, cells, table, psf):
    return pl.pallas_call(
        pack_kernel,
        name="pack",
        out_shape=[
            jax.ShapeDtypeStruct((TOTAL, BLK, N), BF),
            jax.ShapeDtypeStruct((TOTAL, MAPS), BF),
            jax.ShapeDtypeStruct((2 * TOTAL, MAPS), F32),
        ],
        in_specs=[SMEM_SPEC, SMEM_SPEC, VMEM_SPEC, ANY_SPEC],
        out_specs=[ANY_SPEC, VMEM_SPEC, VMEM_SPEC],
        scratch_shapes=[
            pltpu.VMEM((SLOT + 1, BLK, N), BF),
            pltpu.SemaphoreType.DMA,
            pltpu.SemaphoreType.DMA((TOTAL,)),
        ],
        compiler_params=params(8),
    )(counts, cells, table, psf)


CHUNKS = 8


def pupil_kernel(
    counts_ref, bands_ref, coef_ref, seeds_ref, maps_ref, sent_ref, frac_ref, cos_ref, sin_ref,
    maps, spread, field, path, sem,
):
    group = lax.axis_index("star")
    depth = MAPS * BLK // CHUNKS
    loads = []
    for c in range(CHUNKS):
        rows = pl.ds(c * depth, depth)
        load = pltpu.make_async_copy(maps_ref.at[rows], maps.at[rows], sem.at[c])
        load.start()
        loads.append(load)
    mine = jnp.where(iota((MINE * BLK, TOTAL), 1) == group * MINE + iota((MINE * BLK, TOTAL), 0) // BLK, 1.0, 0.0)
    rows = dot(mine.astype(BF), coef_ref[...]).astype(BF)
    for c in range(CHUNKS):
        k = iota((MAPS, depth), 0)
        each = jnp.where(k == (c * depth + iota((MAPS, depth), 1)) // BLK, 1.0, 0.0).astype(BF)
        wide = dot(rows, each)
        same = iota(wide.shape, 0) % BLK == iota(wide.shape, 1) % BLK
        spread[:, c * depth : (c + 1) * depth] = jnp.where(same, wide, 0.0).astype(BF)

    def table_rows(a, carry):
        ca, sa = seeds_ref[1, 0, pl.ds(a, 1), :], seeds_ref[1, 1, pl.ds(a, 1), :]
        cb, sb = seeds_ref[0, 0], seeds_ref[0, 1]
        at = pl.ds(pl.multiple_of(a * 32, 32), 32)
        cos_ref[at, :] = (ca * cb - sa * sb).astype(BF)
        sin_ref[at, :] = (ca * sb + sa * cb).astype(BF)
        return carry

    lax.fori_loop(0, 32, table_rows, 0)
    for c in range(CHUNKS):
        loads[c].wait()
        part = dot(spread[:, c * depth : (c + 1) * depth], maps[c * depth : (c + 1) * depth, :])
        path[...] = part if c == 0 else path[...] + part
    bands = my_bands(counts_ref, bands_ref, group)
    first = lax.axis_index("row") * BLK
    for j in range(MINE):
        turn = pick(TURNS, bands[j])
        for h in range(BLK // 16):
            at = slice(j * BLK + h * 16, j * BLK + h * 16 + 16)
            t = path[at, :] * turn
            f = t - jnp.round(t)
            frac_ref[at, :] = f
            c, s = cos_sin_turns(f)
            inside = aperture_mask(first + h * 16, 16)
            field[at, :] = jnp.where(inside, c, 0.0).astype(BF)
            field[slice(at.start + 128, at.stop + 128), :] = jnp.where(inside, s, 0.0).astype(BF)
    for m in range(4):
        at = slice(m * 256, m * 256 + 256)
        by_cos = dot(cos_ref[at, :], field[...], NT)
        by_sin = dot(sin_ref[at, :], field[...], NT)
        sent_ref[at, :128] = (by_cos[:, :128] - by_sin[:, 128:]).astype(BF)
        sent_ref[at, 128:] = (by_sin[:, :128] + by_cos[:, 128:]).astype(BF)


def pupil(counts, bands, coef, seeds, maps):
    return pl.pallas_call(
        pupil_kernel,
        name="pupil",
        out_shape=[
            jax.ShapeDtypeStruct((N, 256), BF),
            jax.ShapeDtypeStruct((MINE * BLK, N), F32),
            jax.ShapeDtypeStruct((N, N), BF),
            jax.ShapeDtypeStruct((N, N), BF),
        ],
        in_specs=[SMEM_SPEC, SMEM_SPEC, VMEM_SPEC, VMEM_SPEC, ANY_SPEC],
        out_specs=[VMEM_SPEC] * 4,
        scratch_shapes=[
            pltpu.VMEM((MAPS * BLK, N), BF),
            pltpu.VMEM((MINE * BLK, MAPS * BLK), BF),
            pltpu.VMEM((256, N), BF),
            pltpu.VMEM((MINE * BLK, N), F32),
            pltpu.SemaphoreType.DMA((CHUNKS,)),
        ],
        compiler_params=params(32),
    )(counts, bands, coef, seeds, maps)


def gather_blocks(got_ref, out_ref):
    lane = iota((BLK, 128), 1)
    low = lane < 64
    even = lane % 64 < 32
    for part in range(2):
        for quad in range(8):
            x = [
                got_ref[(4 * quad + i) * BLK : (4 * quad + i + 1) * BLK, part * 128 : part * 128 + 128].astype(F32)
                for i in range(4)
            ]
            y = [None] * 4
            for i in range(2):
                y[i] = jnp.where(low, x[i], pltpu.roll(x[i + 2], 64, 1))
                y[i + 2] = jnp.where(low, pltpu.roll(x[i], 64, 1), x[i + 2])
            z = [None] * 4
            for i in (0, 2):
                z[i] = jnp.where(even, y[i], pltpu.roll(y[i + 1], 32, 1))
                z[i + 1] = jnp.where(even, pltpu.roll(y[i], 96, 1), y[i + 1])
            for s in range(4):
                at = part * 128 + s * BLK
                out_ref[at : at + BLK, quad * 128 : quad * 128 + 128] = z[s].astype(BF)


def focal_kernel(got_ref, cos_ref, sin_ref, cot_ref, sent_ref, field, grad):
    gather_blocks(got_ref, field)
    for n in range(4):
        at = slice(n * 256, n * 256 + 256)
        by_cos = dot(field[...], cos_ref[:, at])
        by_sin = dot(field[...], sin_ref[:, at])
        weight = cot_ref[:, at].astype(F32) * (2.0 / N)
        grad[:128, at] = (weight * (by_cos[:128] - by_sin[128:])).astype(BF)
        grad[128:, at] = (weight * (by_sin[:128] + by_cos[128:])).astype(BF)
    for m in range(4):
        at = slice(m * 256, m * 256 + 256)
        by_cos = dot(cos_ref[at, :], grad[...], NT)
        by_sin = dot(sin_ref[at, :], grad[...], NT)
        sent_ref[at, :128] = ((by_cos[:, :128] + by_sin[:, 128:]) * (1.0 / N)).astype(BF)
        sent_ref[at, 128:] = ((by_cos[:, 128:] - by_sin[:, :128]) * (1.0 / N)).astype(BF)


def focal(got, cos_table, sin_table, cot):
    return pl.pallas_call(
        focal_kernel,
        name="focal",
        out_shape=jax.ShapeDtypeStruct((N, 256), BF),
        in_specs=[VMEM_SPEC] * 4,
        out_specs=VMEM_SPEC,
        scratch_shapes=[pltpu.VMEM((256, N), BF), pltpu.VMEM((256, N), BF)],
        compiler_params=params(24),
    )(got, cos_table, sin_table, cot)


def back_kernel(
    counts_ref, bands_ref, got_ref, cos_ref, sin_ref, frac_ref, maps_ref, path_grad_ref, score_ref,
    maps, field, sem,
):
    group = lax.axis_index("star")
    load = pltpu.make_async_copy(maps_ref, maps, sem)
    load.start()
    gather_blocks(got_ref, field)
    bands = my_bands(counts_ref, bands_ref, group)
    first = lax.axis_index("row") * BLK
    inside = aperture_mask(first, BLK)
    waves = [pick(WAVES, b) for b in bands]
    for n in range(4):
        at = slice(n * 256, n * 256 + 256)
        by_cos = dot(field[...], cos_ref[:, at])
        by_sin = dot(field[...], sin_ref[:, at])
        real = by_cos[:128] + by_sin[128:]
        imag = by_cos[128:] - by_sin[:128]
        for j in range(MINE):
            rows = slice(j * BLK, j * BLK + BLK)
            c, s = cos_sin_turns(frac_ref[rows, at])
            grad = waves[j] * (c * imag[rows] - s * real[rows])
            path_grad_ref[rows, at] = jnp.where(inside[:, at], grad, 0.0).astype(BF)
    load.wait()
    parts = []
    for c in range(8):
        some = dot(maps[c * 256 : (c + 1) * 256, :], path_grad_ref[...], NT)
        same = iota(some.shape, 0) % BLK == iota(some.shape, 1) % BLK
        kept = jnp.where(same, some, 0.0)
        for k in range(8):
            parts.append(jnp.sum(kept[k * BLK : (k + 1) * BLK], axis=0, keepdims=True))
    by_lane = jnp.concatenate(parts, axis=0)
    pick_star = jnp.where(iota((8, 128), 1) // BLK == iota((8, 128), 0), 1.0, 0.0)
    scores = dot(pick_star, by_lane, NT, lax.Precision.HIGHEST)
    wide = jnp.concatenate([scores, jnp.zeros_like(scores)], axis=1)
    score_ref[...] = jnp.broadcast_to(wide[None], score_ref.shape)


def back(counts, bands, got, cos_table, sin_table, frac, maps):
    return pl.pallas_call(
        back_kernel,
        name="back",
        out_shape=[
            jax.ShapeDtypeStruct((MINE * BLK, N), BF),
            jax.ShapeDtypeStruct((32, 8, 128), F32),
        ],
        in_specs=[SMEM_SPEC, SMEM_SPEC, VMEM_SPEC, VMEM_SPEC, VMEM_SPEC, VMEM_SPEC, ANY_SPEC],
        out_specs=[VMEM_SPEC, VMEM_SPEC],
        scratch_shapes=[
            pltpu.VMEM((MAPS * BLK, N), BF),
            pltpu.VMEM((256, N), BF),
            pltpu.SemaphoreType.DMA,
        ],
        compiler_params=params(32),
    )(counts, bands, got, cos_table, sin_table, frac, maps)


def total_kernel(coef_ref, hot_ref, path_grad_ref, score_ref, map_grad_ref, coef_grad_ref):
    group = lax.axis_index("star")
    share = MAPS // GROUPS
    mine = jnp.where(iota((share * BLK, MAPS), 1) == group * share + iota((share * BLK, MAPS), 0) // BLK, 1.0, 0.0)
    rows = dot(mine.astype(BF), coef_ref[...], NT).astype(BF)
    each = jnp.where(iota((TOTAL, N), 0) == iota((TOTAL, N), 1) // BLK, 1.0, 0.0).astype(BF)
    wide = dot(rows, each)
    same = iota(wide.shape, 0) % BLK == iota(wide.shape, 1) % BLK
    spread = jnp.where(same, wide, 0.0).astype(BF)
    map_grad_ref[...] = dot(spread, path_grad_ref[...])
    scores = score_ref[...].reshape(64, 128)
    grad = dot(hot_ref[...], scores, TN, lax.Precision.HIGHEST) * (1.0 / (8 * N))
    coef_grad_ref[...] = grad[:, :MAPS]


def total(coef, hot, path_grads, scores):
    return pl.pallas_call(
        total_kernel,
        name="total",
        out_shape=[
            jax.ShapeDtypeStruct((MAPS // GROUPS * BLK, N), F32),
            jax.ShapeDtypeStruct((64, MAPS), F32),
        ],
        in_specs=[VMEM_SPEC] * 4,
        out_specs=[VMEM_SPEC, VMEM_SPEC],
        compiler_params=params(24),
    )(coef, hot, path_grads, scores)


def per_device(feature_maps, coef_table, star_counts, star_cells, star_bands, psf_cotangent):
    maps = feature_maps.reshape(MAPS * BLK, N)
    packed, coef, hot = pack(star_counts, star_cells, coef_table, psf_cotangent)
    cot = lax.psum_scatter(packed, "star", scatter_dimension=0, tiled=True).reshape(MINE * BLK, N)
    sent, frac, cos_table, sin_table = pupil(star_counts, star_bands, coef, jnp.asarray(table_seeds()), maps)
    got = lax.all_to_all(sent.reshape(32, BLK, 256), "row", 0, 0, tiled=True).reshape(N, 256)
    sent = focal(got, cos_table, sin_table, cot)
    got = lax.all_to_all(sent.reshape(32, BLK, 256), "row", 0, 0, tiled=True).reshape(N, 256)
    path_grad, score = back(star_counts, star_bands, got, cos_table, sin_table, frac, maps)
    path_grads = lax.all_gather(path_grad, "star", axis=0, tiled=True)
    score = lax.all_to_all(score, "row", 0, 0, tiled=True)
    score = jnp.broadcast_to(jnp.sum(score, 0)[None], (GROUPS, 8, 128))
    score = lax.all_to_all(score, "star", 0, 0, tiled=True)
    map_grad, coef_grad = total(coef, hot, path_grads, score)
    return map_grad.reshape(MAPS // GROUPS, BLK, N), coef_grad


def solution(mesh):
    placed = (P(None, "row", None), P(), P(), P(), P(), P("star", "row", None))
    return jax.shard_map(
        per_device,
        mesh=mesh,
        in_specs=placed,
        out_specs=(P("star", "row", None), P()),
        check_vma=False,
    )
```

```python
import jax
import jax.numpy as jnp
import numpy as np
from jax import lax
from jax.experimental import pallas as pl
from jax.experimental.pallas import tpu as pltpu
from jax.sharding import PartitionSpec as P

BF = jnp.bfloat16
F32 = jnp.float32
N = 1024
MAPS = 64
BLK = 32
GROUPS = 8
SLOT = 12
TOTAL = 32
MINE = 4
WAVES = [float(np.float32(2.0 * np.pi) / np.float32(0.55 + 0.35 * b / 7)) for b in range(8)]
TURNS = [float(1.0 / (0.55 + 0.35 * b / 7)) for b in range(8)]
VMEM_SPEC = pl.BlockSpec(memory_space=pltpu.VMEM)
SMEM_SPEC = pl.BlockSpec(memory_space=pltpu.SMEM)
HBM_SPEC = pl.BlockSpec(memory_space=pltpu.HBM)
ANY_SPEC = pl.BlockSpec(memory_space=pl.ANY)
NN = (((1,), (0,)), ((), ()))
NT = (((1,), (1,)), ((), ()))
TN = (((0,), (0,)), ((), ()))


def dot(a, b, dims=NN, precision=None):
    return lax.dot_general(a, b, dims, precision=precision, preferred_element_type=F32)


def iota(shape, axis):
    return lax.broadcasted_iota(jnp.int32, shape, axis)


def in_hbm(*arrays):
    return [pltpu.with_memory_space_constraint(a, pltpu.HBM) for a in arrays]


def params(mib):
    return pltpu.CompilerParams(vmem_limit_bytes=mib << 20)


def table_seeds():
    b = np.arange(N, dtype=np.int64)
    low = (np.arange(32)[:, None] * b[None, :]) % N
    high = (32 * (np.arange(32) % 16)[:, None] * b[None, :]) % N
    both = np.stack([low, high]) * (2.0 * np.pi / N)
    return np.stack([np.cos(both), -np.sin(both)], 1).astype(np.float32)


def fit_polynomials():
    x = 0.125 * (1.0 + np.cos(np.pi * (np.arange(4000) + 0.5) / 4000))
    f = np.sqrt(x)
    cheb = np.polynomial.chebyshev.Chebyshev
    poly = np.polynomial.polynomial.Polynomial
    c = cheb.fit(x, np.cos(2 * np.pi * f), 7, domain=[0, 0.25]).convert(kind=poly)
    s = cheb.fit(x, np.sin(2 * np.pi * f) / f, 6, domain=[0, 0.25]).convert(kind=poly)
    return [float(v) for v in c.coef], [float(v) for v in s.coef]


COS_POLY, SIN_POLY = fit_polynomials()


def cos_sin_turns(f):
    x = f * f
    c = jnp.full_like(f, COS_POLY[-1])
    s = jnp.full_like(f, SIN_POLY[-1])
    for a in COS_POLY[-2::-1]:
        c = c * x + a
    for a in SIN_POLY[-2::-1]:
        s = s * x + a
    return c, s * f


def assigned(h, t, counts):
    before, count, free = jnp.zeros_like(h), jnp.zeros_like(h), jnp.int32(0)
    for g in range(GROUPS):
        before = jnp.where(h == g, free, before)
        count = jnp.where(h == g, counts[g], count)
        free = free + jnp.maximum(MINE - counts[g], 0)
    e = before + t - count
    slot, first = jnp.zeros_like(h), jnp.int32(0)
    for g in range(GROUPS):
        after = first + jnp.maximum(counts[g] - MINE, 0)
        slot = jnp.where((e >= first) & (e < after), g * SLOT + MINE + e - first, slot)
        first = after
    return jnp.where(t < count, h * SLOT + t, slot)


def pick(values, index):
    chosen = jnp.float32(values[0])
    for k in range(1, len(values)):
        chosen = jnp.where(index == k, jnp.float32(values[k]), chosen)
    return chosen


def aperture_mask(first_row, rows):
    centre = 0.5 * (N - 1)
    y = (first_row + iota((rows, N), 0)).astype(F32) - centre
    x = iota((rows, N), 1).astype(F32) - centre
    return y * y + x * x <= 0.25 * N * N


def alternate(x):
    return x * jnp.where((iota((1, x.shape[1]), 1) & 1) == 0, 1.0, -1.0)


def same_pixel(shape):
    return ((iota(shape, 0) ^ iota(shape, 1)) & (BLK - 1)) == 0


def times_table(field, table, at):
    upper = dot(field[:, : N // 2], table[:, at])
    lower = dot(field[:, N // 2 :], table[:, at])
    return upper + alternate(lower)


def table_times(tables, both, at):
    return dot(tables[0, at, :], both[...], NT), dot(tables[1, at, :], both[...], NT)


CHUNKS = 2


def pupil_kernel(
    counts_hbm, cells_hbm, bands_hbm, table_hbm, seeds_hbm, maps_hbm,
    sent_hbm, frac_hbm, tables, hot_ref, coef_ref, meta_ref,
    counts_ref, cells_ref, bands_ref, table, seeds, maps, spread, field, path, sent_ref, frac_ref, sem, out_sem,
):
    group = lax.axis_index("star")
    depth = MAPS * BLK // CHUNKS
    small = [
        pltpu.make_async_copy(a, b, sem.at[CHUNKS + i])
        for i, (a, b) in enumerate(
            [(seeds_hbm, seeds), (counts_hbm, counts_ref), (cells_hbm, cells_ref), (bands_hbm, bands_ref), (table_hbm, table)]
        )
    ]
    for copy in small:
        copy.start()
    loads = []
    for c in range(CHUNKS):
        rows = pl.ds(c * depth, depth)
        load = pltpu.make_async_copy(maps_hbm.at[rows], maps.at[rows], sem.at[c])
        load.start()
        loads.append(load)
    small[0].wait()
    cb, sb = seeds[0, 0], seeds[0, 1]
    for a in range(16):
        ca, sa = seeds[1, 0, a : a + 1, :], seeds[1, 1, a : a + 1, :]
        tables[0, a * 32 : a * 32 + 32, :] = (ca * cb - sa * sb).astype(BF)
        tables[1, a * 32 : a * 32 + 32, :] = (ca * sb + sa * cb).astype(BF)
    for copy in small[1:]:
        copy.wait()
    counts = [counts_ref[g] for g in range(GROUPS)]
    place = iota((64, MAPS), 0)
    slots = jnp.where((place & 7) < MINE, assigned(place >> 3, place & 7, counts), -1)
    cell = jnp.full((64, MAPS), -1, jnp.int32)
    for g in range(GROUPS):
        for j in range(SLOT):
            cell = jnp.where(slots == g * SLOT + j, cells_ref[g, j], cell)
    hot = jnp.where(iota((64, MAPS), 1) == cell, 1.0, 0.0)
    hot_ref[...] = hot
    coef_ref[...] = dot(hot.astype(BF), table[...]).astype(BF)
    turns = []
    for t in range(MINE):
        slot = assigned(group, jnp.int32(t), counts)
        band = bands_ref[slot // SLOT, slot % SLOT]
        meta_ref[t] = slot
        meta_ref[MINE + t] = band
        turns.append(pick(TURNS, band))
    for k in range(1, 4):
        other = (group + 2 * k) & 7
        for t in range(1, MINE):
            slot = assigned(other, jnp.int32(t), counts)
            meta_ref[2 * MINE + 3 * (k - 1) + t - 1] = jnp.where((slot // SLOT) >> 1 == group >> 1, slot, -1)
    mine = jnp.where(iota((128, 64), 1) == group * 8 + (iota((128, 64), 0) >> 5), 1.0, 0.0)
    rows = dot(mine.astype(BF), coef_ref[...]).astype(BF)
    same = same_pixel((128, depth))
    k = iota((MAPS, depth), 0)
    for c in range(CHUNKS):
        each = jnp.where(k == c * (MAPS // CHUNKS) + (iota((MAPS, depth), 1) >> 5), 1.0, 0.0).astype(BF)
        wide = dot(rows, each)
        spread[:, c * depth : (c + 1) * depth] = jnp.where(same, wide, 0.0).astype(BF)
    for c in range(CHUNKS):
        loads[c].wait()
        part = dot(spread[:, c * depth : (c + 1) * depth], maps[c * depth : (c + 1) * depth, :])
        path[...] = part if c == 0 else path[...] + part
    first = lax.axis_index("row") * BLK
    for h in range(BLK // 16):
        inside = aperture_mask(first + h * 16, 16)
        for t in range(MINE):
            at = slice(t * BLK + h * 16, t * BLK + h * 16 + 16)
            x = path[at, :] * turns[t]
            f = x - jnp.round(x)
            frac_ref[at, :] = f
            c, s = cos_sin_turns(f)
            for part, value in enumerate((c, s)):
                value = jnp.where(inside, value, 0.0)
                field[slice(at.start + part * 128, at.stop + part * 128), :] = value.astype(BF)
                field[slice(at.start + part * 128 + 256, at.stop + part * 128 + 256), :] = alternate(value).astype(BF)
    stores = [pltpu.make_async_copy(frac_ref, frac_hbm, out_sem.at[4])]
    stores[0].start()
    for m in range(2):
        by_cos, by_sin = table_times(tables, field, slice(m * 256, m * 256 + 256))
        for half in range(2):
            at = slice(half * 512 + m * 256, half * 512 + m * 256 + 256)
            re, im = slice(half * 256, half * 256 + 128), slice(half * 256 + 128, half * 256 + 256)
            sent_ref[at, :128] = (by_cos[:, re] - by_sin[:, im]).astype(BF)
            sent_ref[at, 128:] = (by_sin[:, re] + by_cos[:, im]).astype(BF)
            stores.append(pltpu.make_async_copy(sent_ref.at[at], sent_hbm.at[at], out_sem.at[2 * m + half]))
            stores[-1].start()
    for store in stores:
        store.wait()


def pupil(counts, cells, bands, table, seeds, maps):
    return pl.pallas_call(
        pupil_kernel,
        name="pupil",
        out_shape=[
            pltpu.HBM((N, 256), BF),
            pltpu.HBM((MINE * BLK, N), F32),
            jax.ShapeDtypeStruct((2, N // 2, N), BF),
            jax.ShapeDtypeStruct((64, MAPS), F32),
            jax.ShapeDtypeStruct((64, MAPS), BF),
            jax.ShapeDtypeStruct((2 * MINE + 9,), jnp.int32),
        ],
        in_specs=[HBM_SPEC] * 6,
        out_specs=[HBM_SPEC] * 2 + [VMEM_SPEC] * 3 + [SMEM_SPEC],
        scratch_shapes=[
            pltpu.SMEM((GROUPS,), jnp.int32),
            pltpu.SMEM((GROUPS, SLOT), jnp.int32),
            pltpu.SMEM((GROUPS, SLOT), jnp.int32),
            pltpu.VMEM((64, MAPS), BF),
            pltpu.VMEM((2, 2, 32, N), F32),
            pltpu.VMEM((MAPS * BLK, N), BF),
            pltpu.VMEM((MINE * BLK, MAPS * BLK), BF),
            pltpu.VMEM((512, N), BF),
            pltpu.VMEM((MINE * BLK, N), F32),
            pltpu.VMEM((N, 256), BF),
            pltpu.VMEM((MINE * BLK, N), F32),
            pltpu.SemaphoreType.DMA((CHUNKS + 5,)),
            pltpu.SemaphoreType.DMA((5,)),
        ],
        compiler_params=params(20),
    )(*in_hbm(counts, cells, bands, table, seeds, maps))


def gather_blocks(got_ref, out_ref):
    lane = iota((BLK, 128), 1)
    low = lane < 64
    even = (lane & 63) < 32
    for part in range(2):
        for quad in range(8):
            x = [
                got_ref[(4 * quad + i) * BLK : (4 * quad + i + 1) * BLK, part * 128 : part * 128 + 128].astype(F32)
                for i in range(4)
            ]
            y = [None] * 4
            for i in range(2):
                y[i] = jnp.where(low, x[i], pltpu.roll(x[i + 2], 64, 1))
                y[i + 2] = jnp.where(low, pltpu.roll(x[i], 64, 1), x[i + 2])
            z = [None] * 4
            for i in (0, 2):
                z[i] = jnp.where(even, y[i], pltpu.roll(y[i + 1], 32, 1))
                z[i + 1] = jnp.where(even, pltpu.roll(y[i], 96, 1), y[i + 1])
            for s in range(4):
                at = part * 128 + s * BLK
                out_ref[at : at + BLK, quad * 128 : quad * 128 + 128] = z[s].astype(BF)


def pack_kernel(meta_ref, own_hbm, twin_hbm, one_hbm, two_hbm, three_hbm, sem):
    group = lax.axis_index("star")
    sent = (one_hbm, two_hbm, three_hbm)
    for i in range(9):
        slot = meta_ref[2 * MINE + i]
        place = jnp.maximum(slot, 0) % SLOT
        mine = slot // SLOT == group

        @pl.when((slot >= 0) & mine)
        def _():
            pltpu.make_async_copy(own_hbm.at[place], sent[i // 3].at[i % 3], sem.at[i]).start()

        @pl.when((slot >= 0) & jnp.logical_not(mine))
        def _():
            pltpu.make_async_copy(twin_hbm.at[place], sent[i // 3].at[i % 3], sem.at[i]).start()

    for i in range(9):

        @pl.when(meta_ref[2 * MINE + i] >= 0)
        def _():
            pltpu.make_async_copy(own_hbm.at[0], sent[i // 3].at[i % 3], sem.at[i]).wait()


def pack(meta, own, twin):
    return pl.pallas_call(
        pack_kernel,
        name="pack",
        out_shape=[pltpu.HBM((3, BLK, N), BF)] * 3,
        in_specs=[SMEM_SPEC, HBM_SPEC, ANY_SPEC],
        out_specs=[HBM_SPEC] * 3,
        scratch_shapes=[pltpu.SemaphoreType.DMA((9,))],
        compiler_params=params(4),
    )(meta, *in_hbm(own), twin)


def focal_kernel(
    meta_ref, got_ref, tables, own_hbm, twin_hbm, one_hbm, two_hbm, three_hbm, sent_ref, cot, field, grad, sem
):
    group = lax.axis_index("star")
    for t in range(MINE):
        slot = meta_ref[t]
        owner = slot // SLOT
        place = slot % SLOT
        hop = ((group >> 1) - (owner >> 1)) & 3

        @pl.when((hop == 0) & (owner == group))
        def _():
            pltpu.make_async_copy(own_hbm.at[place], cot.at[t], sem.at[t]).start()

        @pl.when((hop == 0) & (owner != group))
        def _():
            pltpu.make_async_copy(twin_hbm.at[place], cot.at[t], sem.at[t]).start()

        for k, got in ((1, one_hbm), (2, two_hbm), (3, three_hbm)):

            @pl.when(hop == k)
            def _():
                pltpu.make_async_copy(got.at[max(t - 1, 0)], cot.at[t], sem.at[t]).start()

    gather_blocks(got_ref, field)
    for n in range(4):
        at = slice(n * 256, n * 256 + 256)
        by_cos = times_table(field, tables.at[0], at)
        by_sin = times_table(field, tables.at[1], at)
        if n == 0:
            for t in range(MINE):
                pltpu.make_async_copy(own_hbm.at[t], cot.at[t], sem.at[t]).wait()
        weight = cot[:, :, at].reshape(128, 256).astype(F32) * (2.0 / N)
        for part, value in enumerate((by_cos[:128] - by_sin[128:], by_sin[:128] + by_cos[128:])):
            value = weight * value
            grad[slice(part * 128, part * 128 + 128), at] = value.astype(BF)
            grad[slice(part * 128 + 256, part * 128 + 384), at] = alternate(value).astype(BF)
    for m in range(2):
        by_cos, by_sin = table_times(tables, grad, slice(m * 256, m * 256 + 256))
        for half in range(2):
            at = slice(half * 512 + m * 256, half * 512 + m * 256 + 256)
            re, im = slice(half * 256, half * 256 + 128), slice(half * 256 + 128, half * 256 + 256)
            sent_ref[at, :128] = ((by_cos[:, re] + by_sin[:, im]) * (1.0 / N)).astype(BF)
            sent_ref[at, 128:] = ((by_cos[:, im] - by_sin[:, re]) * (1.0 / N)).astype(BF)


def focal(meta, got, tables, own, twin, moved):
    return pl.pallas_call(
        focal_kernel,
        name="focal",
        out_shape=jax.ShapeDtypeStruct((N, 256), BF),
        in_specs=[SMEM_SPEC, VMEM_SPEC, VMEM_SPEC] + [HBM_SPEC] * 5,
        out_specs=VMEM_SPEC,
        scratch_shapes=[
            pltpu.VMEM((MINE, BLK, N), BF),
            pltpu.VMEM((256, N), BF),
            pltpu.VMEM((512, N), BF),
            pltpu.SemaphoreType.DMA((MINE,)),
        ],
        compiler_params=params(16),
    )(meta, got, tables, *in_hbm(own, twin, *moved))


def back_kernel(meta_ref, got_ref, tables, frac_hbm, path_grad_hbm, path_grad_ref, frac_ref, field, sem, in_sem):
    load = pltpu.make_async_copy(frac_hbm, frac_ref, in_sem)
    load.start()
    gather_blocks(got_ref, field)
    waves = [pick(WAVES, meta_ref[MINE + t]) for t in range(MINE)]
    inside = aperture_mask(lax.axis_index("row") * BLK, BLK)
    copies = []
    for n in range(4):
        at = slice(n * 256, n * 256 + 256)
        by_cos = times_table(field, tables.at[0], at)
        by_sin = times_table(field, tables.at[1], at)
        real = by_cos[:128] + by_sin[128:]
        imag = by_cos[128:] - by_sin[:128]
        if n == 0:
            load.wait()
        for t in range(MINE):
            rows = slice(t * BLK, t * BLK + BLK)
            c, s = cos_sin_turns(frac_ref[rows, at])
            grad = waves[t] * (c * imag[rows] - s * real[rows])
            path_grad_ref[rows, at] = jnp.where(inside[:, at], grad, 0.0).astype(BF)
        copy = pltpu.make_async_copy(path_grad_ref.at[:, at], path_grad_hbm.at[:, at], sem.at[n])
        copy.start()
        copies.append(copy)
    for copy in copies:
        copy.wait()


def back(meta, got, tables, frac):
    return pl.pallas_call(
        back_kernel,
        name="back",
        out_shape=[pltpu.HBM((MINE * BLK, N), BF), jax.ShapeDtypeStruct((MINE * BLK, N), BF)],
        in_specs=[SMEM_SPEC, VMEM_SPEC, VMEM_SPEC, HBM_SPEC],
        out_specs=[HBM_SPEC, VMEM_SPEC],
        scratch_shapes=[
            pltpu.VMEM((MINE * BLK, N), F32),
            pltpu.VMEM((256, N), BF),
            pltpu.SemaphoreType.DMA((4,)),
            pltpu.SemaphoreType.DMA,
        ],
        compiler_params=params(16),
    )(meta, got, tables, *in_hbm(frac))


def score_kernel(path_grad_ref, maps_hbm, score_ref, maps_ref, sem):
    loads = []
    for c in range(2):
        rows = pl.ds(c * 1024, 1024)
        loads.append(pltpu.make_async_copy(maps_hbm.at[rows], maps_ref.at[rows], sem.at[c]))
        loads[-1].start()
    parts = []
    same = same_pixel((256, 128))
    for c in range(8):
        if c % 4 == 0:
            loads[c // 4].wait()
        some = dot(maps_ref[c * 256 : (c + 1) * 256, :], path_grad_ref[...], NT)
        kept = jnp.where(same, some, 0.0)
        for k in range(8):
            parts.append(jnp.sum(kept[k * BLK : (k + 1) * BLK], axis=0, keepdims=True))
    by_lane = jnp.concatenate(parts, axis=0)
    pick_star = jnp.where((iota((8, 128), 1) >> 5) == iota((8, 128), 0), 1.0, 0.0)
    scores = dot(pick_star, by_lane, NT, lax.Precision.HIGHEST)
    wide = jnp.concatenate([scores, jnp.zeros_like(scores)], axis=1)
    score_ref[...] = jnp.broadcast_to(wide[None], score_ref.shape)


def score_of(path_grad, maps):
    return pl.pallas_call(
        score_kernel,
        name="score",
        out_shape=jax.ShapeDtypeStruct((32, 8, 128), F32),
        in_specs=[VMEM_SPEC, HBM_SPEC],
        out_specs=VMEM_SPEC,
        scratch_shapes=[pltpu.VMEM((MAPS * BLK, N), BF), pltpu.SemaphoreType.DMA((2,))],
        compiler_params=params(16),
    )(path_grad, *in_hbm(maps))


def total_kernel(coef_ref, hot_ref, path_grad_hbm, score_ref, map_grad_hbm, coef_grad_ref, path_grad, map_grad, in_sem, out_sem):
    group = lax.axis_index("star")
    loads = []
    for n in range(2):
        at = pl.ds(n * 512, 512)
        load = pltpu.make_async_copy(path_grad_hbm.at[at], path_grad.at[at], in_sem.at[n])
        load.start()
        loads.append(load)
    share = MAPS // GROUPS
    mine = jnp.where(iota((share * BLK, MAPS), 1) == group * share + (iota((share * BLK, MAPS), 0) >> 5), 1.0, 0.0)
    rows = dot(mine.astype(BF), coef_ref[...], NT).astype(BF)
    q = iota((64, N), 1) >> 5
    each = jnp.where(iota((64, N), 0) == ((q >> 2) << 3) + (q & 3), 1.0, 0.0).astype(BF)
    wide = dot(rows, each)
    spread = jnp.where(same_pixel(wide.shape), wide, 0.0).astype(BF)
    stores = []
    for n in range(2):
        loads[n].wait()
        some = slice(n * 512, n * 512 + 512)
        for m in range(2):
            at = slice(m * 128, m * 128 + 128)
            part = dot(spread[at, some], path_grad[some, :])
            map_grad[at, :] = part if n == 0 else map_grad[at, :] + part
            if n == 1:
                store = pltpu.make_async_copy(map_grad.at[at], map_grad_hbm.at[at], out_sem.at[m])
                store.start()
                stores.append(store)
    scores = score_ref[...].reshape(64, 128)
    grad = dot(hot_ref[...], scores, TN, lax.Precision.HIGHEST) * (1.0 / (8 * N))
    coef_grad_ref[...] = grad[:, :MAPS]
    for store in stores:
        store.wait()


def total(coef, hot, path_grads, scores):
    rows = MAPS // GROUPS * BLK
    return pl.pallas_call(
        total_kernel,
        name="total",
        out_shape=[pltpu.HBM((rows, N), F32), jax.ShapeDtypeStruct((64, MAPS), F32)],
        in_specs=[VMEM_SPEC, VMEM_SPEC, HBM_SPEC, VMEM_SPEC],
        out_specs=[HBM_SPEC, VMEM_SPEC],
        scratch_shapes=[
            pltpu.VMEM((N, N), BF),
            pltpu.VMEM((rows, N), F32),
            pltpu.SemaphoreType.DMA((2,)),
            pltpu.SemaphoreType.DMA((2,)),
        ],
        compiler_params=params(16),
    )(coef, hot, *in_hbm(path_grads), scores)


def per_device(feature_maps, coef_table, star_counts, star_cells, star_bands, psf_cotangent):
    maps = feature_maps.reshape(MAPS * BLK, N)
    twin = lax.ppermute(psf_cotangent, "star", [(g, g ^ 1) for g in range(GROUPS)])
    sent, frac, tables, hot, coef, meta = pupil(
        star_counts, star_cells, star_bands, coef_table, jnp.asarray(table_seeds()), maps
    )
    sent, *packed = lax.optimization_barrier((sent, *pack(meta, psf_cotangent, twin)))
    moved = [
        lax.ppermute(packed[k - 1], "star", [(g, (g + 2 * k) % GROUPS) for g in range(GROUPS)]) for k in (1, 2, 3)
    ]
    got = lax.all_to_all(sent.reshape(32, BLK, 256), "row", 0, 0, tiled=True).reshape(N, 256)
    sent = focal(meta, got, tables, psf_cotangent, twin, moved)
    got = lax.all_to_all(sent.reshape(32, BLK, 256), "row", 0, 0, tiled=True).reshape(N, 256)
    path_grad, held = back(meta, got, tables, frac)
    path_grads = lax.all_gather(path_grad, "star", axis=0, tiled=True)
    score = lax.all_to_all(score_of(held, maps), "row", 0, 0, tiled=True)
    score = jnp.broadcast_to(jnp.sum(score, 0)[None], (GROUPS, 8, 128))
    score = lax.all_to_all(score, "star", 0, 0, tiled=True)
    map_grad, coef_grad = total(coef, hot, path_grads, score)
    return map_grad.reshape(MAPS // GROUPS, BLK, N), coef_grad


def solution(mesh):
    placed = (P(None, "row", None), P(), P(), P(), P(), P("star", "row", None))
    return jax.shard_map(
        per_device,
        mesh=mesh,
        in_specs=placed,
        out_specs=(P("star", "row", None), P()),
        check_vma=False,
    )
```

```python
import jax
import jax.numpy as jnp
import numpy as np
from jax import lax
from jax.experimental import pallas as pl
from jax.experimental.pallas import tpu as pltpu
from jax.sharding import PartitionSpec as P

BF = jnp.bfloat16
F32 = jnp.float32
N = 1024
MAPS = 64
BLK = 32
GROUPS = 8
SLOT = 12
TOTAL = 32
MINE = 4
WAVES = [float(np.float32(2.0 * np.pi) / np.float32(0.55 + 0.35 * b / 7)) for b in range(8)]
TURNS = [float(1.0 / (0.55 + 0.35 * b / 7)) for b in range(8)]
VMEM_SPEC = pl.BlockSpec(memory_space=pltpu.VMEM)
SMEM_SPEC = pl.BlockSpec(memory_space=pltpu.SMEM)
HBM_SPEC = pl.BlockSpec(memory_space=pltpu.HBM)
ANY_SPEC = pl.BlockSpec(memory_space=pl.ANY)
NN = (((1,), (0,)), ((), ()))
NT = (((1,), (1,)), ((), ()))
TN = (((0,), (0,)), ((), ()))


def dot(a, b, dims=NN, precision=None):
    return lax.dot_general(a, b, dims, precision=precision, preferred_element_type=F32)


def iota(shape, axis):
    return lax.broadcasted_iota(jnp.int32, shape, axis)


def in_hbm(*arrays):
    return [pltpu.with_memory_space_constraint(a, pltpu.HBM) for a in arrays]


def params(mib):
    return pltpu.CompilerParams(vmem_limit_bytes=mib << 20)


def table_seeds():
    b = np.arange(N, dtype=np.int64)
    low = (np.arange(32)[:, None] * b[None, :]) % N
    high = (32 * (np.arange(32) % 16)[:, None] * b[None, :]) % N
    both = np.stack([low, high]) * (2.0 * np.pi / N)
    return np.stack([np.cos(both), -np.sin(both)], 1).astype(np.float32)


def fit_polynomials():
    x = 0.125 * (1.0 + np.cos(np.pi * (np.arange(4000) + 0.5) / 4000))
    f = np.sqrt(x)
    cheb = np.polynomial.chebyshev.Chebyshev
    poly = np.polynomial.polynomial.Polynomial
    c = cheb.fit(x, np.cos(2 * np.pi * f), 7, domain=[0, 0.25]).convert(kind=poly)
    s = cheb.fit(x, np.sin(2 * np.pi * f) / f, 6, domain=[0, 0.25]).convert(kind=poly)
    return [float(v) for v in c.coef], [float(v) for v in s.coef]


COS_POLY, SIN_POLY = fit_polynomials()


def cos_sin_turns(f):
    x = f * f
    c = jnp.full_like(f, COS_POLY[-1])
    s = jnp.full_like(f, SIN_POLY[-1])
    for a in COS_POLY[-2::-1]:
        c = c * x + a
    for a in SIN_POLY[-2::-1]:
        s = s * x + a
    return c, s * f


def assigned(h, t, counts):
    before, count, free = jnp.zeros_like(h), jnp.zeros_like(h), jnp.int32(0)
    for g in range(GROUPS):
        before = jnp.where(h == g, free, before)
        count = jnp.where(h == g, counts[g], count)
        free = free + jnp.maximum(MINE - counts[g], 0)
    e = before + t - count
    slot, first = jnp.zeros_like(h), jnp.int32(0)
    for g in range(GROUPS):
        after = first + jnp.maximum(counts[g] - MINE, 0)
        slot = jnp.where((e >= first) & (e < after), g * SLOT + MINE + e - first, slot)
        first = after
    return jnp.where(t < count, h * SLOT + t, slot)


def pick(values, index):
    chosen = jnp.float32(values[0])
    for k in range(1, len(values)):
        chosen = jnp.where(index == k, jnp.float32(values[k]), chosen)
    return chosen


def aperture_mask(first_row, rows):
    centre = 0.5 * (N - 1)
    y = (first_row + iota((rows, N), 0)).astype(F32) - centre
    x = iota((rows, N), 1).astype(F32) - centre
    return y * y + x * x <= 0.25 * N * N


def alternate(x):
    return x * jnp.where((iota((1, x.shape[1]), 1) & 1) == 0, 1.0, -1.0)


def same_pixel(shape):
    return ((iota(shape, 0) ^ iota(shape, 1)) & (BLK - 1)) == 0


def times_table(field, table, at):
    upper = dot(field[:, : N // 2], table[:, at])
    lower = dot(field[:, N // 2 :], table[:, at])
    return upper + alternate(lower)


def table_times(tables, both, at):
    return dot(tables[0, at, :], both[...], NT), dot(tables[1, at, :], both[...], NT)


CHUNKS = 2


def pupil_kernel(
    counts_hbm, cells_hbm, bands_hbm, table_hbm, seeds_hbm, maps_hbm,
    sent_hbm, frac_hbm, tables, hot_ref, coef_ref, meta_ref,
    counts_ref, cells_ref, bands_ref, table, seeds, maps, spread, field, path, sent_ref, frac_ref, sem, out_sem,
):
    group = lax.axis_index("star")
    depth = MAPS * BLK // CHUNKS
    small = [
        pltpu.make_async_copy(a, b, sem.at[CHUNKS + i])
        for i, (a, b) in enumerate(
            [(seeds_hbm, seeds), (counts_hbm, counts_ref), (cells_hbm, cells_ref), (bands_hbm, bands_ref), (table_hbm, table)]
        )
    ]
    for copy in small:
        copy.start()
    loads = []
    for c in range(CHUNKS):
        rows = pl.ds(c * depth, depth)
        load = pltpu.make_async_copy(maps_hbm.at[rows], maps.at[rows], sem.at[c])
        load.start()
        loads.append(load)
    small[0].wait()
    cb, sb = seeds[0, 0], seeds[0, 1]
    for a in range(16):
        ca, sa = seeds[1, 0, a : a + 1, :], seeds[1, 1, a : a + 1, :]
        tables[0, a * 32 : a * 32 + 32, :] = (ca * cb - sa * sb).astype(BF)
        tables[1, a * 32 : a * 32 + 32, :] = (ca * sb + sa * cb).astype(BF)
    for copy in small[1:]:
        copy.wait()
    counts = [counts_ref[g] for g in range(GROUPS)]
    place = iota((64, MAPS), 0)
    slots = jnp.where((place & 7) < MINE, assigned(place >> 3, place & 7, counts), -1)
    cell = jnp.full((64, MAPS), -1, jnp.int32)
    for g in range(GROUPS):
        for j in range(SLOT):
            cell = jnp.where(slots == g * SLOT + j, cells_ref[g, j], cell)
    hot = jnp.where(iota((64, MAPS), 1) == cell, 1.0, 0.0)
    hot_ref[...] = hot
    coef_ref[...] = dot(hot.astype(BF), table[...]).astype(BF)
    turns = []
    for t in range(MINE):
        slot = assigned(group, jnp.int32(t), counts)
        band = bands_ref[slot // SLOT, slot % SLOT]
        meta_ref[t] = slot
        meta_ref[MINE + t] = band
        turns.append(pick(TURNS, band))
    for k in range(1, 4):
        other = (group + 2 * k) & 7
        for t in range(1, MINE):
            slot = assigned(other, jnp.int32(t), counts)
            meta_ref[2 * MINE + 3 * (k - 1) + t - 1] = jnp.where((slot // SLOT) >> 1 == group >> 1, slot, -1)
    mine = jnp.where(iota((128, 64), 1) == group * 8 + (iota((128, 64), 0) >> 5), 1.0, 0.0)
    rows = dot(mine.astype(BF), coef_ref[...]).astype(BF)
    same = same_pixel((128, depth))
    k = iota((MAPS, depth), 0)
    for c in range(CHUNKS):
        each = jnp.where(k == c * (MAPS // CHUNKS) + (iota((MAPS, depth), 1) >> 5), 1.0, 0.0).astype(BF)
        wide = dot(rows, each)
        spread[:, c * depth : (c + 1) * depth] = jnp.where(same, wide, 0.0).astype(BF)
    for c in range(CHUNKS):
        loads[c].wait()
        part = dot(spread[:, c * depth : (c + 1) * depth], maps[c * depth : (c + 1) * depth, :])
        path[...] = part if c == 0 else path[...] + part
    first = lax.axis_index("row") * BLK
    for h in range(BLK // 16):
        inside = aperture_mask(first + h * 16, 16)
        for t in range(MINE):
            at = slice(t * BLK + h * 16, t * BLK + h * 16 + 16)
            x = path[at, :] * turns[t]
            f = x - jnp.round(x)
            frac_ref[at, :] = f
            c, s = cos_sin_turns(f)
            for part, value in enumerate((c, s)):
                value = jnp.where(inside, value, 0.0)
                field[slice(at.start + part * 128, at.stop + part * 128), :] = value.astype(BF)
                field[slice(at.start + part * 128 + 256, at.stop + part * 128 + 256), :] = alternate(value).astype(BF)
    stores = [pltpu.make_async_copy(frac_ref, frac_hbm, out_sem.at[4])]
    stores[0].start()
    for m in range(2):
        by_cos, by_sin = table_times(tables, field, slice(m * 256, m * 256 + 256))
        for half in range(2):
            at = slice(half * 512 + m * 256, half * 512 + m * 256 + 256)
            re, im = slice(half * 256, half * 256 + 128), slice(half * 256 + 128, half * 256 + 256)
            sent_ref[at, :128] = (by_cos[:, re] - by_sin[:, im]).astype(BF)
            sent_ref[at, 128:] = (by_sin[:, re] + by_cos[:, im]).astype(BF)
            stores.append(pltpu.make_async_copy(sent_ref.at[at], sent_hbm.at[at], out_sem.at[2 * m + half]))
            stores[-1].start()
    for store in stores:
        store.wait()


def pupil(counts, cells, bands, table, seeds, maps):
    return pl.pallas_call(
        pupil_kernel,
        name="pupil",
        out_shape=[
            pltpu.HBM((N, 256), BF),
            pltpu.HBM((MINE * BLK, N), F32),
            jax.ShapeDtypeStruct((2, N // 2, N), BF),
            jax.ShapeDtypeStruct((64, MAPS), F32),
            jax.ShapeDtypeStruct((64, MAPS), BF),
            jax.ShapeDtypeStruct((2 * MINE + 9,), jnp.int32),
        ],
        in_specs=[HBM_SPEC] * 6,
        out_specs=[HBM_SPEC] * 2 + [VMEM_SPEC] * 3 + [SMEM_SPEC],
        scratch_shapes=[
            pltpu.SMEM((GROUPS,), jnp.int32),
            pltpu.SMEM((GROUPS, SLOT), jnp.int32),
            pltpu.SMEM((GROUPS, SLOT), jnp.int32),
            pltpu.VMEM((64, MAPS), BF),
            pltpu.VMEM((2, 2, 32, N), F32),
            pltpu.VMEM((MAPS * BLK, N), BF),
            pltpu.VMEM((MINE * BLK, MAPS * BLK), BF),
            pltpu.VMEM((512, N), BF),
            pltpu.VMEM((MINE * BLK, N), F32),
            pltpu.VMEM((N, 256), BF),
            pltpu.VMEM((MINE * BLK, N), F32),
            pltpu.SemaphoreType.DMA((CHUNKS + 5,)),
            pltpu.SemaphoreType.DMA((5,)),
        ],
        compiler_params=params(20),
    )(*in_hbm(counts, cells, bands, table, seeds, maps))


def gather_blocks(got_ref, out_ref):
    lane = iota((BLK, 128), 1)
    low = lane < 64
    even = (lane & 63) < 32
    for part in range(2):
        for quad in range(8):
            x = [
                got_ref[(4 * quad + i) * BLK : (4 * quad + i + 1) * BLK, part * 128 : part * 128 + 128].astype(F32)
                for i in range(4)
            ]
            y = [None] * 4
            for i in range(2):
                y[i] = jnp.where(low, x[i], pltpu.roll(x[i + 2], 64, 1))
                y[i + 2] = jnp.where(low, pltpu.roll(x[i], 64, 1), x[i + 2])
            z = [None] * 4
            for i in (0, 2):
                z[i] = jnp.where(even, y[i], pltpu.roll(y[i + 1], 32, 1))
                z[i + 1] = jnp.where(even, pltpu.roll(y[i], 96, 1), y[i + 1])
            for s in range(4):
                at = part * 128 + s * BLK
                out_ref[at : at + BLK, quad * 128 : quad * 128 + 128] = z[s].astype(BF)


def pack_kernel(meta_ref, own_hbm, twin_hbm, one_hbm, two_hbm, three_hbm, sem):
    group = lax.axis_index("star")
    sent = (one_hbm, two_hbm, three_hbm)
    for i in range(9):
        slot = meta_ref[2 * MINE + i]
        place = jnp.maximum(slot, 0) % SLOT
        mine = slot // SLOT == group

        @pl.when((slot >= 0) & mine)
        def _():
            pltpu.make_async_copy(own_hbm.at[place], sent[i // 3].at[i % 3], sem.at[i]).start()

        @pl.when((slot >= 0) & jnp.logical_not(mine))
        def _():
            pltpu.make_async_copy(twin_hbm.at[place], sent[i // 3].at[i % 3], sem.at[i]).start()

    for i in range(9):

        @pl.when(meta_ref[2 * MINE + i] >= 0)
        def _():
            pltpu.make_async_copy(own_hbm.at[0], sent[i // 3].at[i % 3], sem.at[i]).wait()


def pack(meta, own, twin):
    return pl.pallas_call(
        pack_kernel,
        name="pack",
        out_shape=[pltpu.HBM((3, BLK, N), BF)] * 3,
        in_specs=[SMEM_SPEC, HBM_SPEC, ANY_SPEC],
        out_specs=[HBM_SPEC] * 3,
        scratch_shapes=[pltpu.SemaphoreType.DMA((9,))],
        compiler_params=params(4),
    )(meta, *in_hbm(own), twin)


def focal_kernel(
    meta_ref, got_ref, tables, own_hbm, twin_hbm, one_hbm, two_hbm, three_hbm, sent_ref, cot, field, grad, sem
):
    group = lax.axis_index("star")
    for t in range(MINE):
        slot = meta_ref[t]
        owner = slot // SLOT
        place = slot % SLOT
        hop = ((group >> 1) - (owner >> 1)) & 3

        @pl.when((hop == 0) & (owner == group))
        def _():
            pltpu.make_async_copy(own_hbm.at[place], cot.at[t], sem.at[t]).start()

        @pl.when((hop == 0) & (owner != group))
        def _():
            pltpu.make_async_copy(twin_hbm.at[place], cot.at[t], sem.at[t]).start()

        for k, got in ((1, one_hbm), (2, two_hbm), (3, three_hbm)):

            @pl.when(hop == k)
            def _():
                pltpu.make_async_copy(got.at[max(t - 1, 0)], cot.at[t], sem.at[t]).start()

    gather_blocks(got_ref, field)
    for n in range(4):
        at = slice(n * 256, n * 256 + 256)
        by_cos = times_table(field, tables.at[0], at)
        by_sin = times_table(field, tables.at[1], at)
        if n == 0:
            for t in range(MINE):
                pltpu.make_async_copy(own_hbm.at[t], cot.at[t], sem.at[t]).wait()
        weight = cot[:, :, at].reshape(128, 256).astype(F32) * (2.0 / N)
        for part, value in enumerate((by_cos[:128] - by_sin[128:], by_sin[:128] + by_cos[128:])):
            value = weight * value
            grad[slice(part * 128, part * 128 + 128), at] = value.astype(BF)
            grad[slice(part * 128 + 256, part * 128 + 384), at] = alternate(value).astype(BF)
    for m in range(2):
        by_cos, by_sin = table_times(tables, grad, slice(m * 256, m * 256 + 256))
        for half in range(2):
            at = slice(half * 512 + m * 256, half * 512 + m * 256 + 256)
            re, im = slice(half * 256, half * 256 + 128), slice(half * 256 + 128, half * 256 + 256)
            sent_ref[at, :128] = ((by_cos[:, re] + by_sin[:, im]) * (1.0 / N)).astype(BF)
            sent_ref[at, 128:] = ((by_cos[:, im] - by_sin[:, re]) * (1.0 / N)).astype(BF)


def focal(meta, got, tables, own, twin, moved):
    return pl.pallas_call(
        focal_kernel,
        name="focal",
        out_shape=jax.ShapeDtypeStruct((N, 256), BF),
        in_specs=[SMEM_SPEC, VMEM_SPEC, VMEM_SPEC] + [HBM_SPEC] * 5,
        out_specs=VMEM_SPEC,
        scratch_shapes=[
            pltpu.VMEM((MINE, BLK, N), BF),
            pltpu.VMEM((256, N), BF),
            pltpu.VMEM((512, N), BF),
            pltpu.SemaphoreType.DMA((MINE,)),
        ],
        compiler_params=params(16),
    )(meta, got, tables, *in_hbm(own, twin, *moved))


def back_kernel(meta_ref, got_ref, tables, frac_hbm, path_grad_ref, frac_ref, field, in_sem):
    load = pltpu.make_async_copy(frac_hbm, frac_ref, in_sem)
    load.start()
    gather_blocks(got_ref, field)
    waves = [pick(WAVES, meta_ref[MINE + t]) for t in range(MINE)]
    inside = aperture_mask(lax.axis_index("row") * BLK, BLK)
    for n in range(4):
        at = slice(n * 256, n * 256 + 256)
        by_cos = times_table(field, tables.at[0], at)
        by_sin = times_table(field, tables.at[1], at)
        real = by_cos[:128] + by_sin[128:]
        imag = by_cos[128:] - by_sin[:128]
        if n == 0:
            load.wait()
        for t in range(MINE):
            rows = slice(t * BLK, t * BLK + BLK)
            c, s = cos_sin_turns(frac_ref[rows, at])
            grad = waves[t] * (c * imag[rows] - s * real[rows])
            path_grad_ref[rows, at] = jnp.where(inside[:, at], grad, 0.0).astype(BF)


def back(meta, got, tables, frac):
    return pl.pallas_call(
        back_kernel,
        name="back",
        out_shape=jax.ShapeDtypeStruct((MINE * BLK, N), BF),
        in_specs=[SMEM_SPEC, VMEM_SPEC, VMEM_SPEC, HBM_SPEC],
        out_specs=VMEM_SPEC,
        scratch_shapes=[
            pltpu.VMEM((MINE * BLK, N), F32),
            pltpu.VMEM((256, N), BF),
            pltpu.SemaphoreType.DMA,
        ],
        compiler_params=params(16),
    )(meta, got, tables, *in_hbm(frac))


def score_kernel(path_grad_ref, maps_hbm, score_ref, maps_ref, sem):
    loads = []
    for c in range(2):
        rows = pl.ds(c * 1024, 1024)
        loads.append(pltpu.make_async_copy(maps_hbm.at[rows], maps_ref.at[rows], sem.at[c]))
        loads[-1].start()
    parts = []
    same = same_pixel((256, 128))
    for c in range(8):
        if c % 4 == 0:
            loads[c // 4].wait()
        some = dot(maps_ref[c * 256 : (c + 1) * 256, :], path_grad_ref[...], NT)
        kept = jnp.where(same, some, 0.0)
        for k in range(8):
            parts.append(jnp.sum(kept[k * BLK : (k + 1) * BLK], axis=0, keepdims=True))
    by_lane = jnp.concatenate(parts, axis=0)
    pick_star = jnp.where((iota((8, 128), 1) >> 5) == iota((8, 128), 0), 1.0, 0.0)
    scores = dot(pick_star, by_lane, NT, lax.Precision.HIGHEST)
    wide = jnp.concatenate([scores, jnp.zeros_like(scores)], axis=1)
    score_ref[...] = jnp.broadcast_to(wide[None], score_ref.shape)


def score_of(path_grad, maps):
    return pl.pallas_call(
        score_kernel,
        name="score",
        out_shape=jax.ShapeDtypeStruct((32, 8, 128), F32),
        in_specs=[VMEM_SPEC, HBM_SPEC],
        out_specs=VMEM_SPEC,
        scratch_shapes=[pltpu.VMEM((MAPS * BLK, N), BF), pltpu.SemaphoreType.DMA((2,))],
        compiler_params=params(16),
    )(path_grad, *in_hbm(maps))


def total_kernel(coef_ref, hot_ref, score_ref, *refs):
    blocks = refs[: 2 * MINE]
    map_grad_hbm, coef_grad_ref, path_grad, map_grad, out_sem = refs[2 * MINE :]
    group = lax.axis_index("star")
    for i, block in enumerate(blocks):
        h = (group ^ (i // MINE)) - 2 * (i % MINE) & (GROUPS - 1)
        path_grad[pl.ds(pl.multiple_of(h * 128, 128), 128), :] = block[...]
    share = MAPS // GROUPS
    mine = jnp.where(iota((share * BLK, MAPS), 1) == group * share + (iota((share * BLK, MAPS), 0) >> 5), 1.0, 0.0)
    rows = dot(mine.astype(BF), coef_ref[...], NT).astype(BF)
    q = iota((64, N), 1) >> 5
    each = jnp.where(iota((64, N), 0) == ((q >> 2) << 3) + (q & 3), 1.0, 0.0).astype(BF)
    wide = dot(rows, each)
    spread = jnp.where(same_pixel(wide.shape), wide, 0.0).astype(BF)
    stores = []
    for m in range(2):
        at = slice(m * 128, m * 128 + 128)
        map_grad[at, :] = dot(spread[at], path_grad[...])
        store = pltpu.make_async_copy(map_grad.at[at], map_grad_hbm.at[at], out_sem.at[m])
        store.start()
        stores.append(store)
    scores = score_ref[...].reshape(64, 128)
    grad = dot(hot_ref[...], scores, TN, lax.Precision.HIGHEST) * (1.0 / (8 * N))
    coef_grad_ref[...] = grad[:, :MAPS]
    for store in stores:
        store.wait()


def total(coef, hot, scores, blocks):
    rows = MAPS // GROUPS * BLK
    return pl.pallas_call(
        total_kernel,
        name="total",
        out_shape=[pltpu.HBM((rows, N), F32), jax.ShapeDtypeStruct((64, MAPS), F32)],
        in_specs=[VMEM_SPEC] * 11,
        out_specs=[HBM_SPEC, VMEM_SPEC],
        scratch_shapes=[
            pltpu.VMEM((N, N), BF),
            pltpu.VMEM((rows, N), F32),
            pltpu.SemaphoreType.DMA((2,)),
        ],
        compiler_params=params(16),
    )(coef, hot, scores, *blocks)


def swap_cores(x):
    return lax.ppermute(x, "star", [(g, g ^ 1) for g in range(GROUPS)])


def along_x(x, k):
    return lax.ppermute(x, "star", [(g, (g + 2 * k) % GROUPS) for g in range(GROUPS)])


def per_device(feature_maps, coef_table, star_counts, star_cells, star_bands, psf_cotangent):
    maps = feature_maps.reshape(MAPS * BLK, N)
    twin = swap_cores(psf_cotangent)
    sent, frac, tables, hot, coef, meta = pupil(
        star_counts, star_cells, star_bands, coef_table, jnp.asarray(table_seeds()), maps
    )
    sent, *packed = lax.optimization_barrier((sent, *pack(meta, psf_cotangent, twin)))
    moved = [along_x(packed[k - 1], k) for k in (1, 2, 3)]
    got = lax.all_to_all(sent.reshape(32, BLK, 256), "row", 0, 0, tiled=True).reshape(N, 256)
    sent = focal(meta, got, tables, psf_cotangent, twin, moved)
    got = lax.all_to_all(sent.reshape(32, BLK, 256), "row", 0, 0, tiled=True).reshape(N, 256)
    path_grad = back(meta, got, tables, frac)
    blocks = [path_grad] + [along_x(path_grad, k) for k in (1, 2, 3)]
    score = lax.all_to_all(score_of(path_grad, maps), "row", 0, 0, tiled=True)
    score, *blocks = lax.optimization_barrier((score, *blocks))
    blocks = blocks + [swap_cores(block) for block in blocks]
    score = jnp.broadcast_to(jnp.sum(score, 0)[None], (GROUPS, 8, 128))
    score = lax.all_to_all(score, "star", 0, 0, tiled=True)
    map_grad, coef_grad = total(coef, hot, score, blocks)
    return map_grad.reshape(MAPS // GROUPS, BLK, N), coef_grad


def solution(mesh):
    placed = (P(None, "row", None), P(), P(), P(), P(), P("star", "row", None))
    return jax.shard_map(
        per_device,
        mesh=mesh,
        in_specs=placed,
        out_specs=(P("star", "row", None), P()),
        check_vma=False,
    )
```

```python
import jax
import jax.numpy as jnp
import numpy as np
from jax import lax
from jax.experimental import pallas as pl
from jax.experimental.pallas import tpu as pltpu
from jax.sharding import PartitionSpec as P

BF = jnp.bfloat16
F32 = jnp.float32
N = 1024
MAPS = 64
BLK = 32
GROUPS = 8
SLOT = 12
TOTAL = 32
MINE = 4
WAVES = [float(np.float32(2.0 * np.pi) / np.float32(0.55 + 0.35 * b / 7)) for b in range(8)]
TURNS = [float(1.0 / (0.55 + 0.35 * b / 7)) for b in range(8)]
VMEM_SPEC = pl.BlockSpec(memory_space=pltpu.VMEM)
SMEM_SPEC = pl.BlockSpec(memory_space=pltpu.SMEM)
HBM_SPEC = pl.BlockSpec(memory_space=pltpu.HBM)
ANY_SPEC = pl.BlockSpec(memory_space=pl.ANY)
NN = (((1,), (0,)), ((), ()))
NT = (((1,), (1,)), ((), ()))
TN = (((0,), (0,)), ((), ()))


def dot(a, b, dims=NN, precision=None):
    return lax.dot_general(a, b, dims, precision=precision, preferred_element_type=F32)


def iota(shape, axis):
    return lax.broadcasted_iota(jnp.int32, shape, axis)


def in_hbm(*arrays):
    return [pltpu.with_memory_space_constraint(a, pltpu.HBM) for a in arrays]


def params(mib):
    return pltpu.CompilerParams(vmem_limit_bytes=mib << 20)


def table_seeds():
    b = np.arange(N, dtype=np.int64)
    low = (np.arange(32)[:, None] * b[None, :]) % N
    high = (32 * (np.arange(32) % 16)[:, None] * b[None, :]) % N
    both = np.stack([low, high]) * (2.0 * np.pi / N)
    return np.stack([np.cos(both), -np.sin(both)], 1).astype(np.float32)


def fit_polynomials():
    x = 0.125 * (1.0 + np.cos(np.pi * (np.arange(4000) + 0.5) / 4000))
    f = np.sqrt(x)
    cheb = np.polynomial.chebyshev.Chebyshev
    poly = np.polynomial.polynomial.Polynomial
    c = cheb.fit(x, np.cos(2 * np.pi * f), 7, domain=[0, 0.25]).convert(kind=poly)
    s = cheb.fit(x, np.sin(2 * np.pi * f) / f, 6, domain=[0, 0.25]).convert(kind=poly)
    return [float(v) for v in c.coef], [float(v) for v in s.coef]


COS_POLY, SIN_POLY = fit_polynomials()


def cos_sin_turns(f):
    x = f * f
    c = jnp.full_like(f, COS_POLY[-1])
    s = jnp.full_like(f, SIN_POLY[-1])
    for a in COS_POLY[-2::-1]:
        c = c * x + a
    for a in SIN_POLY[-2::-1]:
        s = s * x + a
    return c, s * f


def assigned(h, t, counts):
    before, count, free = jnp.zeros_like(h), jnp.zeros_like(h), jnp.int32(0)
    for g in range(GROUPS):
        before = jnp.where(h == g, free, before)
        count = jnp.where(h == g, counts[g], count)
        free = free + jnp.maximum(MINE - counts[g], 0)
    e = before + t - count
    slot, first = jnp.zeros_like(h), jnp.int32(0)
    for g in range(GROUPS):
        after = first + jnp.maximum(counts[g] - MINE, 0)
        slot = jnp.where((e >= first) & (e < after), g * SLOT + MINE + e - first, slot)
        first = after
    return jnp.where(t < count, h * SLOT + t, slot)


def pick(values, index):
    chosen = jnp.float32(values[0])
    for k in range(1, len(values)):
        chosen = jnp.where(index == k, jnp.float32(values[k]), chosen)
    return chosen


def aperture_mask(first_row, rows):
    centre = 0.5 * (N - 1)
    y = (first_row + iota((rows, N), 0)).astype(F32) - centre
    x = iota((rows, N), 1).astype(F32) - centre
    return y * y + x * x <= 0.25 * N * N


def alternate(x):
    return x * jnp.where((iota((1, x.shape[1]), 1) & 1) == 0, 1.0, -1.0)


def same_pixel(shape):
    return ((iota(shape, 0) ^ iota(shape, 1)) & (BLK - 1)) == 0


def times_table(field, table, at):
    upper = dot(field[:, : N // 2], table[:, at])
    lower = dot(field[:, N // 2 :], table[:, at])
    return upper + alternate(lower)


def table_times(tables, both, at):
    return dot(tables[0, at, :], both[...], NT), dot(tables[1, at, :], both[...], NT)


CHUNKS = 2


def pupil_kernel(
    counts_hbm, cells_hbm, bands_hbm, table_hbm, seeds_hbm, maps_hbm,
    sent_hbm, frac_hbm, tables, hot_ref, coef_ref, meta_ref,
    counts_ref, cells_ref, bands_ref, table, seeds, maps, spread, field, path, sent_ref, frac_ref, sem, out_sem,
):
    group = lax.axis_index("star")
    depth = MAPS * BLK // CHUNKS
    small = [
        pltpu.make_async_copy(a, b, sem.at[CHUNKS + i])
        for i, (a, b) in enumerate(
            [(seeds_hbm, seeds), (counts_hbm, counts_ref), (cells_hbm, cells_ref), (bands_hbm, bands_ref), (table_hbm, table)]
        )
    ]
    for copy in small:
        copy.start()
    loads = []
    for c in range(CHUNKS):
        rows = pl.ds(c * depth, depth)
        load = pltpu.make_async_copy(maps_hbm.at[rows], maps.at[rows], sem.at[c])
        load.start()
        loads.append(load)
    small[0].wait()
    cb, sb = seeds[0, 0], seeds[0, 1]
    for a in range(16):
        ca, sa = seeds[1, 0, a : a + 1, :], seeds[1, 1, a : a + 1, :]
        tables[0, a * 32 : a * 32 + 32, :] = (ca * cb - sa * sb).astype(BF)
        tables[1, a * 32 : a * 32 + 32, :] = (ca * sb + sa * cb).astype(BF)
    for copy in small[1:]:
        copy.wait()
    counts = [counts_ref[g] for g in range(GROUPS)]
    place = iota((64, MAPS), 0)
    slots = jnp.where((place & 7) < MINE, assigned(place >> 3, place & 7, counts), -1)
    cell = jnp.full((64, MAPS), -1, jnp.int32)
    for g in range(GROUPS):
        for j in range(SLOT):
            cell = jnp.where(slots == g * SLOT + j, cells_ref[g, j], cell)
    hot = jnp.where(iota((64, MAPS), 1) == cell, 1.0, 0.0)
    hot_ref[...] = hot
    coef_ref[...] = dot(hot.astype(BF), table[...]).astype(BF)
    turns = []
    for t in range(MINE):
        slot = assigned(group, jnp.int32(t), counts)
        band = bands_ref[slot // SLOT, slot % SLOT]
        meta_ref[t] = slot
        meta_ref[MINE + t] = band
        turns.append(pick(TURNS, band))
    for k in range(1, 4):
        other = (group + 2 * k) & 7
        for t in range(1, MINE):
            slot = assigned(other, jnp.int32(t), counts)
            meta_ref[2 * MINE + 3 * (k - 1) + t - 1] = jnp.where((slot // SLOT) >> 1 == group >> 1, slot, -1)
    mine = jnp.where(iota((128, 64), 1) == group * 8 + (iota((128, 64), 0) >> 5), 1.0, 0.0)
    rows = dot(mine.astype(BF), coef_ref[...]).astype(BF)
    same = same_pixel((128, depth))
    k = iota((MAPS, depth), 0)
    for c in range(CHUNKS):
        each = jnp.where(k == c * (MAPS // CHUNKS) + (iota((MAPS, depth), 1) >> 5), 1.0, 0.0).astype(BF)
        wide = dot(rows, each)
        spread[:, c * depth : (c + 1) * depth] = jnp.where(same, wide, 0.0).astype(BF)
    for c in range(CHUNKS):
        loads[c].wait()
        part = dot(spread[:, c * depth : (c + 1) * depth], maps[c * depth : (c + 1) * depth, :])
        path[...] = part if c == 0 else path[...] + part
    first = lax.axis_index("row") * BLK
    for h in range(BLK // 16):
        inside = aperture_mask(first + h * 16, 16)
        for t in range(MINE):
            at = slice(t * BLK + h * 16, t * BLK + h * 16 + 16)
            x = path[at, :] * turns[t]
            f = x - jnp.round(x)
            frac_ref[at, :] = f
            c, s = cos_sin_turns(f)
            for part, value in enumerate((c, s)):
                value = jnp.where(inside, value, 0.0)
                field[slice(at.start + part * 128, at.stop + part * 128), :] = value.astype(BF)
                field[slice(at.start + part * 128 + 256, at.stop + part * 128 + 256), :] = alternate(value).astype(BF)
    stores = [pltpu.make_async_copy(frac_ref, frac_hbm, out_sem.at[4])]
    stores[0].start()
    for m in range(2):
        by_cos, by_sin = table_times(tables, field, slice(m * 256, m * 256 + 256))
        for half in range(2):
            at = slice(half * 512 + m * 256, half * 512 + m * 256 + 256)
            re, im = slice(half * 256, half * 256 + 128), slice(half * 256 + 128, half * 256 + 256)
            sent_ref[at, :128] = (by_cos[:, re] - by_sin[:, im]).astype(BF)
            sent_ref[at, 128:] = (by_sin[:, re] + by_cos[:, im]).astype(BF)
            stores.append(pltpu.make_async_copy(sent_ref.at[at], sent_hbm.at[at], out_sem.at[2 * m + half]))
            stores[-1].start()
    for store in stores:
        store.wait()


def pupil(counts, cells, bands, table, seeds, maps):
    return pl.pallas_call(
        pupil_kernel,
        name="pupil",
        out_shape=[
            pltpu.HBM((N, 256), BF),
            pltpu.HBM((MINE * BLK, N), F32),
            jax.ShapeDtypeStruct((2, N // 2, N), BF),
            jax.ShapeDtypeStruct((64, MAPS), F32),
            jax.ShapeDtypeStruct((64, MAPS), BF),
            jax.ShapeDtypeStruct((2 * MINE + 9,), jnp.int32),
        ],
        in_specs=[HBM_SPEC] * 6,
        out_specs=[HBM_SPEC] * 2 + [VMEM_SPEC] * 3 + [SMEM_SPEC],
        scratch_shapes=[
            pltpu.SMEM((GROUPS,), jnp.int32),
            pltpu.SMEM((GROUPS, SLOT), jnp.int32),
            pltpu.SMEM((GROUPS, SLOT), jnp.int32),
            pltpu.VMEM((64, MAPS), BF),
            pltpu.VMEM((2, 2, 32, N), F32),
            pltpu.VMEM((MAPS * BLK, N), BF),
            pltpu.VMEM((MINE * BLK, MAPS * BLK), BF),
            pltpu.VMEM((512, N), BF),
            pltpu.VMEM((MINE * BLK, N), F32),
            pltpu.VMEM((N, 256), BF),
            pltpu.VMEM((MINE * BLK, N), F32),
            pltpu.SemaphoreType.DMA((CHUNKS + 5,)),
            pltpu.SemaphoreType.DMA((5,)),
        ],
        compiler_params=params(20),
    )(*in_hbm(counts, cells, bands, table, seeds, maps))


def gather_blocks(got_ref, out_ref):
    lane = iota((BLK, 128), 1)
    low = lane < 64
    even = (lane & 63) < 32
    for part in range(2):
        for quad in range(8):
            x = [
                got_ref[(4 * quad + i) * BLK : (4 * quad + i + 1) * BLK, part * 128 : part * 128 + 128].astype(F32)
                for i in range(4)
            ]
            y = [None] * 4
            for i in range(2):
                y[i] = jnp.where(low, x[i], pltpu.roll(x[i + 2], 64, 1))
                y[i + 2] = jnp.where(low, pltpu.roll(x[i], 64, 1), x[i + 2])
            z = [None] * 4
            for i in (0, 2):
                z[i] = jnp.where(even, y[i], pltpu.roll(y[i + 1], 32, 1))
                z[i + 1] = jnp.where(even, pltpu.roll(y[i], 96, 1), y[i + 1])
            for s in range(4):
                at = part * 128 + s * BLK
                out_ref[at : at + BLK, quad * 128 : quad * 128 + 128] = z[s].astype(BF)


def pack_kernel(meta_ref, own_hbm, twin_hbm, one_hbm, two_hbm, three_hbm, held, in_sem, out_sem):
    group = lax.axis_index("star")
    sent = (one_hbm, two_hbm, three_hbm)
    for i in range(9):
        slot = meta_ref[2 * MINE + i]
        place = jnp.maximum(slot, 0) % SLOT
        mine = slot // SLOT == group

        @pl.when((slot >= 0) & mine)
        def _():
            pltpu.make_async_copy(own_hbm.at[place], held.at[i], in_sem.at[i]).start()

        @pl.when((slot >= 0) & jnp.logical_not(mine))
        def _():
            pltpu.make_async_copy(twin_hbm.at[place], held.at[i], in_sem.at[i]).start()

    for i in range(9):

        @pl.when(meta_ref[2 * MINE + i] >= 0)
        def _():
            pltpu.make_async_copy(own_hbm.at[0], held.at[i], in_sem.at[i]).wait()
            pltpu.make_async_copy(held.at[i], sent[i // 3].at[i % 3], out_sem.at[i]).start()

    for i in range(9):

        @pl.when(meta_ref[2 * MINE + i] >= 0)
        def _():
            pltpu.make_async_copy(held.at[i], sent[i // 3].at[i % 3], out_sem.at[i]).wait()


def pack(meta, own, twin):
    return pl.pallas_call(
        pack_kernel,
        name="pack",
        out_shape=[pltpu.HBM((3, BLK, N), BF)] * 3,
        in_specs=[SMEM_SPEC, HBM_SPEC, ANY_SPEC],
        out_specs=[HBM_SPEC] * 3,
        scratch_shapes=[
            pltpu.VMEM((9, BLK, N), BF),
            pltpu.SemaphoreType.DMA((9,)),
            pltpu.SemaphoreType.DMA((9,)),
        ],
        compiler_params=params(4),
    )(meta, *in_hbm(own), twin)


def focal_kernel(
    meta_ref, got_ref, tables, own_hbm, twin_hbm, one_hbm, two_hbm, three_hbm, sent_ref, cot, field, grad, sem
):
    group = lax.axis_index("star")
    for t in range(MINE):
        slot = meta_ref[t]
        owner = slot // SLOT
        place = slot % SLOT
        hop = ((group >> 1) - (owner >> 1)) & 3

        @pl.when((hop == 0) & (owner == group))
        def _():
            pltpu.make_async_copy(own_hbm.at[place], cot.at[t], sem.at[t]).start()

        @pl.when((hop == 0) & (owner != group))
        def _():
            pltpu.make_async_copy(twin_hbm.at[place], cot.at[t], sem.at[t]).start()

        for k, got in ((1, one_hbm), (2, two_hbm), (3, three_hbm)):

            @pl.when(hop == k)
            def _():
                pltpu.make_async_copy(got.at[max(t - 1, 0)], cot.at[t], sem.at[t]).start()

    gather_blocks(got_ref, field)
    for n in range(4):
        at = slice(n * 256, n * 256 + 256)
        by_cos = times_table(field, tables.at[0], at)
        by_sin = times_table(field, tables.at[1], at)
        if n == 0:
            for t in range(MINE):
                pltpu.make_async_copy(own_hbm.at[t], cot.at[t], sem.at[t]).wait()
        weight = cot[:, :, at].reshape(128, 256).astype(F32) * (2.0 / N)
        for part, value in enumerate((by_cos[:128] - by_sin[128:], by_sin[:128] + by_cos[128:])):
            value = weight * value
            grad[slice(part * 128, part * 128 + 128), at] = value.astype(BF)
            grad[slice(part * 128 + 256, part * 128 + 384), at] = alternate(value).astype(BF)
    for m in range(2):
        by_cos, by_sin = table_times(tables, grad, slice(m * 256, m * 256 + 256))
        for half in range(2):
            at = slice(half * 512 + m * 256, half * 512 + m * 256 + 256)
            re, im = slice(half * 256, half * 256 + 128), slice(half * 256 + 128, half * 256 + 256)
            sent_ref[at, :128] = ((by_cos[:, re] + by_sin[:, im]) * (1.0 / N)).astype(BF)
            sent_ref[at, 128:] = ((by_cos[:, im] - by_sin[:, re]) * (1.0 / N)).astype(BF)


def focal(meta, got, tables, own, twin, moved):
    return pl.pallas_call(
        focal_kernel,
        name="focal",
        out_shape=jax.ShapeDtypeStruct((N, 256), BF),
        in_specs=[SMEM_SPEC, VMEM_SPEC, VMEM_SPEC] + [HBM_SPEC] * 5,
        out_specs=VMEM_SPEC,
        scratch_shapes=[
            pltpu.VMEM((MINE, BLK, N), BF),
            pltpu.VMEM((256, N), BF),
            pltpu.VMEM((512, N), BF),
            pltpu.SemaphoreType.DMA((MINE,)),
        ],
        compiler_params=params(16),
    )(meta, got, tables, *in_hbm(own, twin, *moved))


def back_kernel(meta_ref, got_ref, tables, frac_hbm, path_grad_ref, frac_ref, field, in_sem):
    load = pltpu.make_async_copy(frac_hbm, frac_ref, in_sem)
    load.start()
    gather_blocks(got_ref, field)
    waves = [pick(WAVES, meta_ref[MINE + t]) for t in range(MINE)]
    inside = aperture_mask(lax.axis_index("row") * BLK, BLK)
    for n in range(4):
        at = slice(n * 256, n * 256 + 256)
        by_cos = times_table(field, tables.at[0], at)
        by_sin = times_table(field, tables.at[1], at)
        real = by_cos[:128] + by_sin[128:]
        imag = by_cos[128:] - by_sin[:128]
        if n == 0:
            load.wait()
        for t in range(MINE):
            rows = slice(t * BLK, t * BLK + BLK)
            c, s = cos_sin_turns(frac_ref[rows, at])
            grad = waves[t] * (c * imag[rows] - s * real[rows])
            path_grad_ref[rows, at] = jnp.where(inside[:, at], grad, 0.0).astype(BF)


def back(meta, got, tables, frac):
    return pl.pallas_call(
        back_kernel,
        name="back",
        out_shape=jax.ShapeDtypeStruct((MINE * BLK, N), BF),
        in_specs=[SMEM_SPEC, VMEM_SPEC, VMEM_SPEC, HBM_SPEC],
        out_specs=VMEM_SPEC,
        scratch_shapes=[
            pltpu.VMEM((MINE * BLK, N), F32),
            pltpu.VMEM((256, N), BF),
            pltpu.SemaphoreType.DMA,
        ],
        compiler_params=params(16),
    )(meta, got, tables, *in_hbm(frac))


def score_kernel(path_grad_ref, maps_ref, score_ref):
    parts = []
    same = same_pixel((256, 128))
    for c in range(8):
        some = dot(maps_ref[c * 256 : (c + 1) * 256, :], path_grad_ref[...], NT)
        kept = jnp.where(same, some, 0.0)
        for k in range(8):
            parts.append(jnp.sum(kept[k * BLK : (k + 1) * BLK], axis=0, keepdims=True))
    by_lane = jnp.concatenate(parts, axis=0)
    pick_star = jnp.where((iota((8, 128), 1) >> 5) == iota((8, 128), 0), 1.0, 0.0)
    scores = dot(pick_star, by_lane, NT, lax.Precision.HIGHEST)
    wide = jnp.concatenate([scores, jnp.zeros_like(scores)], axis=1)
    score_ref[...] = jnp.broadcast_to(wide[None], score_ref.shape)


def score_of(path_grad, maps):
    return pl.pallas_call(
        score_kernel,
        name="score",
        out_shape=jax.ShapeDtypeStruct((32, 8, 128), F32),
        in_specs=[VMEM_SPEC, VMEM_SPEC],
        out_specs=VMEM_SPEC,
        compiler_params=params(16),
    )(path_grad, maps)


def total_kernel(coef_ref, hot_ref, score_ref, *refs):
    blocks = refs[: 2 * MINE]
    map_grad_hbm, coef_grad_ref, path_grad, map_grad, out_sem = refs[2 * MINE :]
    group = lax.axis_index("star")
    for i, block in enumerate(blocks):
        h = (group ^ (i // MINE)) - 2 * (i % MINE) & (GROUPS - 1)
        path_grad[pl.ds(pl.multiple_of(h * 128, 128), 128), :] = block[...]
    share = MAPS // GROUPS
    mine = jnp.where(iota((share * BLK, MAPS), 1) == group * share + (iota((share * BLK, MAPS), 0) >> 5), 1.0, 0.0)
    rows = dot(mine.astype(BF), coef_ref[...], NT).astype(BF)
    q = iota((64, N), 1) >> 5
    each = jnp.where(iota((64, N), 0) == ((q >> 2) << 3) + (q & 3), 1.0, 0.0).astype(BF)
    wide = dot(rows, each)
    spread = jnp.where(same_pixel(wide.shape), wide, 0.0).astype(BF)
    stores = []
    for m in range(2):
        at = slice(m * 128, m * 128 + 128)
        map_grad[at, :] = dot(spread[at], path_grad[...])
        store = pltpu.make_async_copy(map_grad.at[at], map_grad_hbm.at[at], out_sem.at[m])
        store.start()
        stores.append(store)
    scores = score_ref[...].reshape(64, 128)
    grad = dot(hot_ref[...], scores, TN, lax.Precision.HIGHEST) * (1.0 / (8 * N))
    coef_grad_ref[...] = grad[:, :MAPS]
    for store in stores:
        store.wait()


def total(coef, hot, scores, blocks):
    rows = MAPS // GROUPS * BLK
    return pl.pallas_call(
        total_kernel,
        name="total",
        out_shape=[pltpu.HBM((rows, N), F32), jax.ShapeDtypeStruct((64, MAPS), F32)],
        in_specs=[VMEM_SPEC] * 11,
        out_specs=[HBM_SPEC, VMEM_SPEC],
        scratch_shapes=[
            pltpu.VMEM((N, N), BF),
            pltpu.VMEM((rows, N), F32),
            pltpu.SemaphoreType.DMA((2,)),
        ],
        compiler_params=params(16),
    )(coef, hot, scores, *blocks)


def swap_cores(x):
    return lax.ppermute(x, "star", [(g, g ^ 1) for g in range(GROUPS)])


def along_x(x, k):
    return lax.ppermute(x, "star", [(g, (g + 2 * k) % GROUPS) for g in range(GROUPS)])


def per_device(feature_maps, coef_table, star_counts, star_cells, star_bands, psf_cotangent):
    maps = feature_maps.reshape(MAPS * BLK, N)
    twin = swap_cores(psf_cotangent)
    sent, frac, tables, hot, coef, meta = pupil(
        star_counts, star_cells, star_bands, coef_table, jnp.asarray(table_seeds()), maps
    )
    sent, *packed = lax.optimization_barrier((sent, *pack(meta, psf_cotangent, twin)))
    moved = [along_x(packed[k - 1], k) for k in (1, 2, 3)]
    got = lax.all_to_all(sent.reshape(32, BLK, 256), "row", 0, 0, tiled=True).reshape(N, 256)
    sent = focal(meta, got, tables, psf_cotangent, twin, moved)
    got = lax.all_to_all(sent.reshape(32, BLK, 256), "row", 0, 0, tiled=True).reshape(N, 256)
    path_grad = back(meta, got, tables, frac)
    blocks = [path_grad] + [along_x(path_grad, k) for k in (1, 2, 3)]
    score = lax.all_to_all(score_of(path_grad, maps), "row", 0, 0, tiled=True)
    score, *blocks = lax.optimization_barrier((score, *blocks))
    blocks = blocks + [swap_cores(block) for block in blocks]
    score = jnp.broadcast_to(jnp.sum(score, 0)[None], (GROUPS, 8, 128))
    score = lax.all_to_all(score, "star", 0, 0, tiled=True)
    map_grad, coef_grad = total(coef, hot, score, blocks)
    return map_grad.reshape(MAPS // GROUPS, BLK, N), coef_grad


def solution(mesh):
    placed = (P(None, "row", None), P(), P(), P(), P(), P("star", "row", None))
    return jax.shard_map(
        per_device,
        mesh=mesh,
        in_specs=placed,
        out_specs=(P("star", "row", None), P()),
        check_vma=False,
    )
```

```python
import jax
import jax.numpy as jnp
import numpy as np
from jax import lax
from jax.experimental import pallas as pl
from jax.experimental.pallas import tpu as pltpu
from jax.sharding import PartitionSpec as P

BF = jnp.bfloat16
F32 = jnp.float32
N = 1024
MAPS = 64
BLK = 32
GROUPS = 8
SLOT = 12
TOTAL = 32
MINE = 4
WAVES = [float(np.float32(2.0 * np.pi) / np.float32(0.55 + 0.35 * b / 7)) for b in range(8)]
TURNS = [float(1.0 / (0.55 + 0.35 * b / 7)) for b in range(8)]
VMEM_SPEC = pl.BlockSpec(memory_space=pltpu.VMEM)
SMEM_SPEC = pl.BlockSpec(memory_space=pltpu.SMEM)
HBM_SPEC = pl.BlockSpec(memory_space=pltpu.HBM)
ANY_SPEC = pl.BlockSpec(memory_space=pl.ANY)
NN = (((1,), (0,)), ((), ()))
NT = (((1,), (1,)), ((), ()))
TN = (((0,), (0,)), ((), ()))


def dot(a, b, dims=NN, precision=None):
    return lax.dot_general(a, b, dims, precision=precision, preferred_element_type=F32)


def iota(shape, axis):
    return lax.broadcasted_iota(jnp.int32, shape, axis)


def in_hbm(*arrays):
    return [pltpu.with_memory_space_constraint(a, pltpu.HBM) for a in arrays]


def params(mib):
    return pltpu.CompilerParams(vmem_limit_bytes=mib << 20)


def table_seeds():
    b = np.arange(N, dtype=np.int64)
    low = (np.arange(32)[:, None] * b[None, :]) % N
    high = (32 * (np.arange(32) % 16)[:, None] * b[None, :]) % N
    both = np.stack([low, high]) * (2.0 * np.pi / N)
    return np.stack([np.cos(both), -np.sin(both)], 1).astype(np.float32)


def fit_polynomials():
    x = 0.125 * (1.0 + np.cos(np.pi * (np.arange(4000) + 0.5) / 4000))
    f = np.sqrt(x)
    cheb = np.polynomial.chebyshev.Chebyshev
    poly = np.polynomial.polynomial.Polynomial
    c = cheb.fit(x, np.cos(2 * np.pi * f), 7, domain=[0, 0.25]).convert(kind=poly)
    s = cheb.fit(x, np.sin(2 * np.pi * f) / f, 6, domain=[0, 0.25]).convert(kind=poly)
    return [float(v) for v in c.coef], [float(v) for v in s.coef]


COS_POLY, SIN_POLY = fit_polynomials()


def cos_sin_turns(f):
    x = f * f
    c = jnp.full_like(f, COS_POLY[-1])
    s = jnp.full_like(f, SIN_POLY[-1])
    for a in COS_POLY[-2::-1]:
        c = c * x + a
    for a in SIN_POLY[-2::-1]:
        s = s * x + a
    return c, s * f


def assigned(h, t, counts):
    before, count, free = jnp.zeros_like(h), jnp.zeros_like(h), jnp.int32(0)
    for g in range(GROUPS):
        before = jnp.where(h == g, free, before)
        count = jnp.where(h == g, counts[g], count)
        free = free + jnp.maximum(MINE - counts[g], 0)
    e = before + t - count
    slot, first = jnp.zeros_like(h), jnp.int32(0)
    for g in range(GROUPS):
        after = first + jnp.maximum(counts[g] - MINE, 0)
        slot = jnp.where((e >= first) & (e < after), g * SLOT + MINE + e - first, slot)
        first = after
    return jnp.where(t < count, h * SLOT + t, slot)


def pick(values, index):
    chosen = jnp.float32(values[0])
    for k in range(1, len(values)):
        chosen = jnp.where(index == k, jnp.float32(values[k]), chosen)
    return chosen


def aperture_mask(first_row, rows):
    centre = 0.5 * (N - 1)
    y = (first_row + iota((rows, N), 0)).astype(F32) - centre
    x = iota((rows, N), 1).astype(F32) - centre
    return y * y + x * x <= 0.25 * N * N


def alternate(x):
    return x * jnp.where((iota((1, x.shape[1]), 1) & 1) == 0, 1.0, -1.0)


def same_pixel(shape):
    return ((iota(shape, 0) ^ iota(shape, 1)) & (BLK - 1)) == 0


def times_table(field, table, at):
    upper = dot(field[:, : N // 2], table[:, at])
    lower = dot(field[:, N // 2 :], table[:, at])
    return upper + alternate(lower)


def table_times(tables, both, at):
    return dot(tables[0, at, :], both[...], NT), dot(tables[1, at, :], both[...], NT)


CHUNKS = 2


def pupil_kernel(
    counts_hbm, cells_hbm, bands_hbm, table_hbm, seeds_hbm, maps_hbm,
    sent_hbm, frac_hbm, tables, hot_ref, coef_ref, meta_ref,
    counts_ref, cells_ref, bands_ref, table, seeds, maps, spread, field, path, sent_ref, frac_ref, sem, out_sem,
):
    group = lax.axis_index("star")
    depth = MAPS * BLK // CHUNKS
    small = [
        pltpu.make_async_copy(a, b, sem.at[CHUNKS + i])
        for i, (a, b) in enumerate(
            [(seeds_hbm, seeds), (counts_hbm, counts_ref), (cells_hbm, cells_ref), (bands_hbm, bands_ref), (table_hbm, table)]
        )
    ]
    for copy in small:
        copy.start()
    loads = []
    for c in range(CHUNKS):
        rows = pl.ds(c * depth, depth)
        load = pltpu.make_async_copy(maps_hbm.at[rows], maps.at[rows], sem.at[c])
        load.start()
        loads.append(load)
    small[0].wait()
    cb, sb = seeds[0, 0], seeds[0, 1]
    for a in range(16):
        ca, sa = seeds[1, 0, a : a + 1, :], seeds[1, 1, a : a + 1, :]
        tables[0, a * 32 : a * 32 + 32, :] = (ca * cb - sa * sb).astype(BF)
        tables[1, a * 32 : a * 32 + 32, :] = (ca * sb + sa * cb).astype(BF)
    for copy in small[1:]:
        copy.wait()
    counts = [counts_ref[g] for g in range(GROUPS)]
    place = iota((64, MAPS), 0)
    slots = jnp.where((place & 7) < MINE, assigned(place >> 3, place & 7, counts), -1)
    cell = jnp.full((64, MAPS), -1, jnp.int32)
    for g in range(GROUPS):
        for j in range(SLOT):
            cell = jnp.where(slots == g * SLOT + j, cells_ref[g, j], cell)
    hot = jnp.where(iota((64, MAPS), 1) == cell, 1.0, 0.0)
    hot_ref[...] = hot
    coef_ref[...] = dot(hot.astype(BF), table[...]).astype(BF)
    turns = []
    for t in range(MINE):
        slot = assigned(group, jnp.int32(t), counts)
        band = bands_ref[slot // SLOT, slot % SLOT]
        meta_ref[t] = slot
        meta_ref[MINE + t] = band
        turns.append(pick(TURNS, band))
    for k in range(1, 4):
        other = (group + 2 * k) & 7
        for t in range(1, MINE):
            slot = assigned(other, jnp.int32(t), counts)
            meta_ref[2 * MINE + 3 * (k - 1) + t - 1] = jnp.where((slot // SLOT) >> 1 == group >> 1, slot, -1)
    mine = jnp.where(iota((128, 64), 1) == group * 8 + (iota((128, 64), 0) >> 5), 1.0, 0.0)
    rows = dot(mine.astype(BF), coef_ref[...]).astype(BF)
    same = same_pixel((128, depth))
    k = iota((MAPS, depth), 0)
    for c in range(CHUNKS):
        each = jnp.where(k == c * (MAPS // CHUNKS) + (iota((MAPS, depth), 1) >> 5), 1.0, 0.0).astype(BF)
        wide = dot(rows, each)
        spread[:, c * depth : (c + 1) * depth] = jnp.where(same, wide, 0.0).astype(BF)
    for c in range(CHUNKS):
        loads[c].wait()
        part = dot(spread[:, c * depth : (c + 1) * depth], maps[c * depth : (c + 1) * depth, :])
        path[...] = part if c == 0 else path[...] + part
    first = lax.axis_index("row") * BLK
    for h in range(BLK // 16):
        inside = aperture_mask(first + h * 16, 16)
        for t in range(MINE):
            at = slice(t * BLK + h * 16, t * BLK + h * 16 + 16)
            x = path[at, :] * turns[t]
            f = x - jnp.round(x)
            frac_ref[at, :] = f
            c, s = cos_sin_turns(f)
            for part, value in enumerate((c, s)):
                value = jnp.where(inside, value, 0.0)
                field[slice(at.start + part * 128, at.stop + part * 128), :] = value.astype(BF)
                field[slice(at.start + part * 128 + 256, at.stop + part * 128 + 256), :] = alternate(value).astype(BF)
    stores = [pltpu.make_async_copy(frac_ref, frac_hbm, out_sem.at[4])]
    stores[0].start()
    for m in range(2):
        by_cos, by_sin = table_times(tables, field, slice(m * 256, m * 256 + 256))
        for half in range(2):
            at = slice(half * 512 + m * 256, half * 512 + m * 256 + 256)
            re, im = slice(half * 256, half * 256 + 128), slice(half * 256 + 128, half * 256 + 256)
            sent_ref[at, :128] = (by_cos[:, re] - by_sin[:, im]).astype(BF)
            sent_ref[at, 128:] = (by_sin[:, re] + by_cos[:, im]).astype(BF)
            stores.append(pltpu.make_async_copy(sent_ref.at[at], sent_hbm.at[at], out_sem.at[2 * m + half]))
            stores[-1].start()
    for store in stores:
        store.wait()


def pupil(counts, cells, bands, table, seeds, maps):
    return pl.pallas_call(
        pupil_kernel,
        name="pupil",
        out_shape=[
            pltpu.HBM((N, 256), BF),
            pltpu.HBM((MINE * BLK, N), F32),
            jax.ShapeDtypeStruct((2, N // 2, N), BF),
            jax.ShapeDtypeStruct((64, MAPS), F32),
            jax.ShapeDtypeStruct((64, MAPS), BF),
            jax.ShapeDtypeStruct((2 * MINE + 9,), jnp.int32),
        ],
        in_specs=[HBM_SPEC] * 6,
        out_specs=[HBM_SPEC] * 2 + [VMEM_SPEC] * 3 + [SMEM_SPEC],
        scratch_shapes=[
            pltpu.SMEM((GROUPS,), jnp.int32),
            pltpu.SMEM((GROUPS, SLOT), jnp.int32),
            pltpu.SMEM((GROUPS, SLOT), jnp.int32),
            pltpu.VMEM((64, MAPS), BF),
            pltpu.VMEM((2, 2, 32, N), F32),
            pltpu.VMEM((MAPS * BLK, N), BF),
            pltpu.VMEM((MINE * BLK, MAPS * BLK), BF),
            pltpu.VMEM((512, N), BF),
            pltpu.VMEM((MINE * BLK, N), F32),
            pltpu.VMEM((N, 256), BF),
            pltpu.VMEM((MINE * BLK, N), F32),
            pltpu.SemaphoreType.DMA((CHUNKS + 5,)),
            pltpu.SemaphoreType.DMA((5,)),
        ],
        compiler_params=params(20),
    )(*in_hbm(counts, cells, bands, table, seeds, maps))


def gather_blocks(got_ref, out_ref):
    lane = iota((BLK, 128), 1)
    low = lane < 64
    even = (lane & 63) < 32
    for part in range(2):
        for quad in range(8):
            x = [
                got_ref[(4 * quad + i) * BLK : (4 * quad + i + 1) * BLK, part * 128 : part * 128 + 128].astype(F32)
                for i in range(4)
            ]
            y = [None] * 4
            for i in range(2):
                y[i] = jnp.where(low, x[i], pltpu.roll(x[i + 2], 64, 1))
                y[i + 2] = jnp.where(low, pltpu.roll(x[i], 64, 1), x[i + 2])
            z = [None] * 4
            for i in (0, 2):
                z[i] = jnp.where(even, y[i], pltpu.roll(y[i + 1], 32, 1))
                z[i + 1] = jnp.where(even, pltpu.roll(y[i], 96, 1), y[i + 1])
            for s in range(4):
                at = part * 128 + s * BLK
                out_ref[at : at + BLK, quad * 128 : quad * 128 + 128] = z[s].astype(BF)


def pack_kernel(meta_ref, own_hbm, twin_hbm, one_hbm, two_hbm, three_hbm, held, in_sem, out_sem):
    group = lax.axis_index("star")
    sent = (one_hbm, two_hbm, three_hbm)
    for i in range(9):
        slot = meta_ref[2 * MINE + i]
        place = jnp.maximum(slot, 0) % SLOT
        mine = slot // SLOT == group

        @pl.when((slot >= 0) & mine)
        def _():
            pltpu.make_async_copy(own_hbm.at[place], held.at[i], in_sem.at[i]).start()

        @pl.when((slot >= 0) & jnp.logical_not(mine))
        def _():
            pltpu.make_async_copy(twin_hbm.at[place], held.at[i], in_sem.at[i]).start()

    for i in range(9):

        @pl.when(meta_ref[2 * MINE + i] >= 0)
        def _():
            pltpu.make_async_copy(own_hbm.at[0], held.at[i], in_sem.at[i]).wait()
            pltpu.make_async_copy(held.at[i], sent[i // 3].at[i % 3], out_sem.at[i]).start()

    for i in range(9):

        @pl.when(meta_ref[2 * MINE + i] >= 0)
        def _():
            pltpu.make_async_copy(held.at[i], sent[i // 3].at[i % 3], out_sem.at[i]).wait()


def pack(meta, own, twin):
    return pl.pallas_call(
        pack_kernel,
        name="pack",
        out_shape=[pltpu.HBM((3, BLK, N), BF)] * 3,
        in_specs=[SMEM_SPEC, HBM_SPEC, ANY_SPEC],
        out_specs=[HBM_SPEC] * 3,
        scratch_shapes=[
            pltpu.VMEM((9, BLK, N), BF),
            pltpu.SemaphoreType.DMA((9,)),
            pltpu.SemaphoreType.DMA((9,)),
        ],
        compiler_params=params(4),
    )(meta, *in_hbm(own), twin)


def focal_kernel(
    meta_ref, got_ref, tables, own_hbm, twin_hbm, one_hbm, two_hbm, three_hbm, sent_ref, cot, field, grad, sem
):
    group = lax.axis_index("star")
    for t in range(MINE):
        slot = meta_ref[t]
        owner = slot // SLOT
        place = slot % SLOT
        hop = ((group >> 1) - (owner >> 1)) & 3

        @pl.when((hop == 0) & (owner == group))
        def _():
            pltpu.make_async_copy(own_hbm.at[place], cot.at[t], sem.at[t]).start()

        @pl.when((hop == 0) & (owner != group))
        def _():
            pltpu.make_async_copy(twin_hbm.at[place], cot.at[t], sem.at[t]).start()

        for k, got in ((1, one_hbm), (2, two_hbm), (3, three_hbm)):

            @pl.when(hop == k)
            def _():
                pltpu.make_async_copy(got.at[max(t - 1, 0)], cot.at[t], sem.at[t]).start()

    gather_blocks(got_ref, field)
    for n in range(4):
        at = slice(n * 256, n * 256 + 256)
        by_cos = times_table(field, tables.at[0], at)
        by_sin = times_table(field, tables.at[1], at)
        if n == 0:
            for t in range(MINE):
                pltpu.make_async_copy(own_hbm.at[t], cot.at[t], sem.at[t]).wait()
        weight = cot[:, :, at].reshape(128, 256).astype(F32) * (2.0 / N)
        for part, value in enumerate((by_cos[:128] - by_sin[128:], by_sin[:128] + by_cos[128:])):
            value = weight * value
            grad[slice(part * 128, part * 128 + 128), at] = value.astype(BF)
            grad[slice(part * 128 + 256, part * 128 + 384), at] = alternate(value).astype(BF)
    for m in range(2):
        by_cos, by_sin = table_times(tables, grad, slice(m * 256, m * 256 + 256))
        for half in range(2):
            at = slice(half * 512 + m * 256, half * 512 + m * 256 + 256)
            re, im = slice(half * 256, half * 256 + 128), slice(half * 256 + 128, half * 256 + 256)
            sent_ref[at, :128] = ((by_cos[:, re] + by_sin[:, im]) * (1.0 / N)).astype(BF)
            sent_ref[at, 128:] = ((by_cos[:, im] - by_sin[:, re]) * (1.0 / N)).astype(BF)


def focal(meta, got, tables, own, twin, moved):
    return pl.pallas_call(
        focal_kernel,
        name="focal",
        out_shape=jax.ShapeDtypeStruct((N, 256), BF),
        in_specs=[SMEM_SPEC, VMEM_SPEC, VMEM_SPEC] + [HBM_SPEC] * 5,
        out_specs=VMEM_SPEC,
        scratch_shapes=[
            pltpu.VMEM((MINE, BLK, N), BF),
            pltpu.VMEM((256, N), BF),
            pltpu.VMEM((512, N), BF),
            pltpu.SemaphoreType.DMA((MINE,)),
        ],
        compiler_params=params(16),
    )(meta, got, tables, *in_hbm(own, twin, *moved))


def back_kernel(meta_ref, got_ref, tables, frac_hbm, path_grad_ref, frac_ref, field, in_sem):
    load = pltpu.make_async_copy(frac_hbm, frac_ref, in_sem)
    load.start()
    gather_blocks(got_ref, field)
    waves = [pick(WAVES, meta_ref[MINE + t]) for t in range(MINE)]
    inside = aperture_mask(lax.axis_index("row") * BLK, BLK)
    for n in range(4):
        at = slice(n * 256, n * 256 + 256)
        by_cos = times_table(field, tables.at[0], at)
        by_sin = times_table(field, tables.at[1], at)
        real = by_cos[:128] + by_sin[128:]
        imag = by_cos[128:] - by_sin[:128]
        if n == 0:
            load.wait()
        for t in range(MINE):
            rows = slice(t * BLK, t * BLK + BLK)
            c, s = cos_sin_turns(frac_ref[rows, at])
            grad = waves[t] * (c * imag[rows] - s * real[rows])
            path_grad_ref[rows, at] = jnp.where(inside[:, at], grad, 0.0).astype(BF)


def back(meta, got, tables, frac):
    return pl.pallas_call(
        back_kernel,
        name="back",
        out_shape=jax.ShapeDtypeStruct((MINE * BLK, N), BF),
        in_specs=[SMEM_SPEC, VMEM_SPEC, VMEM_SPEC, HBM_SPEC],
        out_specs=VMEM_SPEC,
        scratch_shapes=[
            pltpu.VMEM((MINE * BLK, N), F32),
            pltpu.VMEM((256, N), BF),
            pltpu.SemaphoreType.DMA,
        ],
        compiler_params=params(16),
    )(meta, got, tables, *in_hbm(frac))


def score_kernel(path_grad_ref, maps_ref, score_ref):
    parts = []
    same = same_pixel((256, 128))
    for c in range(8):
        some = dot(maps_ref[c * 256 : (c + 1) * 256, :], path_grad_ref[...], NT)
        kept = jnp.where(same, some, 0.0)
        for k in range(8):
            parts.append(jnp.sum(kept[k * BLK : (k + 1) * BLK], axis=0, keepdims=True))
    by_lane = jnp.concatenate(parts, axis=0)
    pick_star = jnp.where((iota((8, 128), 1) >> 5) == iota((8, 128), 0), 1.0, 0.0)
    scores = dot(pick_star, by_lane, NT, lax.Precision.HIGHEST)
    wide = jnp.concatenate([scores, jnp.zeros_like(scores)], axis=1)
    score_ref[...] = jnp.broadcast_to(wide[None], score_ref.shape)


def score_of(path_grad, maps):
    return pl.pallas_call(
        score_kernel,
        name="score",
        out_shape=jax.ShapeDtypeStruct((32, 8, 128), F32),
        in_specs=[VMEM_SPEC, VMEM_SPEC],
        out_specs=VMEM_SPEC,
        compiler_params=params(16),
    )(path_grad, maps)


def total_kernel(coef_ref, hot_ref, score_ref, *refs):
    blocks = refs[: 2 * MINE]
    map_grad_hbm, coef_grad_ref, path_grad, map_grad, out_sem = refs[2 * MINE :]
    group = lax.axis_index("star")
    for i, block in enumerate(blocks):
        h = (group ^ (i // MINE)) - 2 * (i % MINE) & (GROUPS - 1)
        path_grad[pl.ds(pl.multiple_of(h * 128, 128), 128), :] = block[...]
    share = MAPS // GROUPS
    mine = jnp.where(iota((share * BLK, MAPS), 1) == group * share + (iota((share * BLK, MAPS), 0) >> 5), 1.0, 0.0)
    rows = dot(mine.astype(BF), coef_ref[...], NT).astype(BF)
    q = iota((64, N), 1) >> 5
    each = jnp.where(iota((64, N), 0) == ((q >> 2) << 3) + (q & 3), 1.0, 0.0).astype(BF)
    wide = dot(rows, each)
    spread = jnp.where(same_pixel(wide.shape), wide, 0.0).astype(BF)
    stores = []
    for m in range(2):
        at = slice(m * 128, m * 128 + 128)
        map_grad[at, :] = dot(spread[at], path_grad[...])
        store = pltpu.make_async_copy(map_grad.at[at], map_grad_hbm.at[at], out_sem.at[m])
        store.start()
        stores.append(store)
    scores = score_ref[...].reshape(64, 128)
    grad = dot(hot_ref[...], scores, TN, lax.Precision.HIGHEST) * (1.0 / (8 * N))
    coef_grad_ref[...] = grad[:, :MAPS]
    for store in stores:
        store.wait()


def total(coef, hot, scores, blocks):
    rows = MAPS // GROUPS * BLK
    return pl.pallas_call(
        total_kernel,
        name="total",
        out_shape=[pltpu.HBM((rows, N), F32), jax.ShapeDtypeStruct((64, MAPS), F32)],
        in_specs=[VMEM_SPEC] * 11,
        out_specs=[HBM_SPEC, VMEM_SPEC],
        scratch_shapes=[
            pltpu.VMEM((N, N), BF),
            pltpu.VMEM((rows, N), F32),
            pltpu.SemaphoreType.DMA((2,)),
        ],
        compiler_params=params(16),
    )(coef, hot, scores, *blocks)


def swap_cores(x):
    return lax.ppermute(x, "star", [(g, g ^ 1) for g in range(GROUPS)])


def along_x(x, k):
    return lax.ppermute(x, "star", [(g, (g + 2 * k) % GROUPS) for g in range(GROUPS)])


def per_device(feature_maps, coef_table, star_counts, star_cells, star_bands, psf_cotangent):
    maps = feature_maps.reshape(MAPS * BLK, N)
    twin = swap_cores(psf_cotangent)
    sent, frac, tables, hot, coef, meta = pupil(
        star_counts, star_cells, star_bands, coef_table, jnp.asarray(table_seeds()), maps
    )
    sent, *packed = lax.optimization_barrier((sent, *pack(meta, psf_cotangent, twin)))
    moved = [along_x(packed[k - 1], k) for k in (1, 2, 3)]
    got = lax.all_to_all(sent.reshape(32, BLK, 256), "row", 0, 0, tiled=True).reshape(N, 256)
    sent = focal(meta, got, tables, psf_cotangent, twin, moved)
    got = lax.all_to_all(sent.reshape(32, BLK, 256), "row", 0, 0, tiled=True).reshape(N, 256)
    path_grad = back(meta, got, tables, frac)
    blocks = [path_grad] + [along_x(path_grad, k) for k in (1, 2, 3)]
    score = lax.all_to_all(score_of(path_grad, maps), "row", 0, 0, tiled=True)
    blocks = blocks + [swap_cores(block) for block in blocks]
    score, blocks[MINE] = lax.optimization_barrier((score, blocks[MINE]))
    score = jnp.broadcast_to(jnp.sum(score, 0)[None], (GROUPS, 8, 128))
    score = lax.all_to_all(score, "star", 0, 0, tiled=True)
    map_grad, coef_grad = total(coef, hot, score, blocks)
    return map_grad.reshape(MAPS // GROUPS, BLK, N), coef_grad


def solution(mesh):
    placed = (P(None, "row", None), P(), P(), P(), P(), P("star", "row", None))
    return jax.shard_map(
        per_device,
        mesh=mesh,
        in_specs=placed,
        out_specs=(P("star", "row", None), P()),
        check_vma=False,
    )
```

```python
import jax
import jax.numpy as jnp
import numpy as np
from jax import lax
from jax.experimental import pallas as pl
from jax.experimental.pallas import tpu as pltpu
from jax.sharding import PartitionSpec as P

BF = jnp.bfloat16
F32 = jnp.float32
N = 1024
MAPS = 64
BLK = 32
GROUPS = 8
SLOT = 12
TOTAL = 32
MINE = 4
WAVES = [float(np.float32(2.0 * np.pi) / np.float32(0.55 + 0.35 * b / 7)) for b in range(8)]
TURNS = [float(1.0 / (0.55 + 0.35 * b / 7)) for b in range(8)]
VMEM_SPEC = pl.BlockSpec(memory_space=pltpu.VMEM)
SMEM_SPEC = pl.BlockSpec(memory_space=pltpu.SMEM)
HBM_SPEC = pl.BlockSpec(memory_space=pltpu.HBM)
ANY_SPEC = pl.BlockSpec(memory_space=pl.ANY)
NN = (((1,), (0,)), ((), ()))
NT = (((1,), (1,)), ((), ()))
TN = (((0,), (0,)), ((), ()))


def dot(a, b, dims=NN, precision=None):
    return lax.dot_general(a, b, dims, precision=precision, preferred_element_type=F32)


def iota(shape, axis):
    return lax.broadcasted_iota(jnp.int32, shape, axis)


def in_hbm(*arrays):
    return [pltpu.with_memory_space_constraint(a, pltpu.HBM) for a in arrays]


def params(mib):
    return pltpu.CompilerParams(vmem_limit_bytes=mib << 20)


def table_seeds():
    b = np.arange(N, dtype=np.int64)
    low = (np.arange(32)[:, None] * b[None, :]) % N
    high = (32 * (np.arange(32) % 16)[:, None] * b[None, :]) % N
    both = np.stack([low, high]) * (2.0 * np.pi / N)
    return np.stack([np.cos(both), -np.sin(both)], 1).astype(np.float32)


def fit_polynomials():
    x = 0.125 * (1.0 + np.cos(np.pi * (np.arange(4000) + 0.5) / 4000))
    f = np.sqrt(x)
    cheb = np.polynomial.chebyshev.Chebyshev
    poly = np.polynomial.polynomial.Polynomial
    c = cheb.fit(x, np.cos(2 * np.pi * f), 7, domain=[0, 0.25]).convert(kind=poly)
    s = cheb.fit(x, np.sin(2 * np.pi * f) / f, 6, domain=[0, 0.25]).convert(kind=poly)
    return [float(v) for v in c.coef], [float(v) for v in s.coef]


COS_POLY, SIN_POLY = fit_polynomials()


def cos_sin_turns(f):
    x = f * f
    c = jnp.full_like(f, COS_POLY[-1])
    s = jnp.full_like(f, SIN_POLY[-1])
    for a in COS_POLY[-2::-1]:
        c = c * x + a
    for a in SIN_POLY[-2::-1]:
        s = s * x + a
    return c, s * f


def assigned(h, t, counts):
    before, count, free = jnp.zeros_like(h), jnp.zeros_like(h), jnp.int32(0)
    for g in range(GROUPS):
        before = jnp.where(h == g, free, before)
        count = jnp.where(h == g, counts[g], count)
        free = free + jnp.maximum(MINE - counts[g], 0)
    e = before + t - count
    slot, first = jnp.zeros_like(h), jnp.int32(0)
    for g in range(GROUPS):
        after = first + jnp.maximum(counts[g] - MINE, 0)
        slot = jnp.where((e >= first) & (e < after), g * SLOT + MINE + e - first, slot)
        first = after
    return jnp.where(t < count, h * SLOT + t, slot)


def pick(values, index):
    chosen = jnp.float32(values[0])
    for k in range(1, len(values)):
        chosen = jnp.where(index == k, jnp.float32(values[k]), chosen)
    return chosen


def aperture_mask(first_row, rows):
    centre = 0.5 * (N - 1)
    y = (first_row + iota((rows, N), 0)).astype(F32) - centre
    x = iota((rows, N), 1).astype(F32) - centre
    return y * y + x * x <= 0.25 * N * N


def alternate(x):
    return x * jnp.where((iota((1, x.shape[1]), 1) & 1) == 0, 1.0, -1.0)


def same_pixel(shape):
    return ((iota(shape, 0) ^ iota(shape, 1)) & (BLK - 1)) == 0


def times_table(field, table, at):
    upper = dot(field[:, : N // 2], table[:, at])
    lower = dot(field[:, N // 2 :], table[:, at])
    return upper + alternate(lower)


def table_times(tables, both, at):
    return dot(tables[0, at, :], both[...], NT), dot(tables[1, at, :], both[...], NT)


CHUNKS = 2


def pupil_kernel(
    counts_hbm, cells_hbm, bands_hbm, table_hbm, seeds_hbm, maps_hbm,
    sent_hbm, frac_hbm, tables, hot_ref, coef_ref, meta_ref,
    counts_ref, cells_ref, bands_ref, table, seeds, maps, spread, field, path, sent_ref, frac_ref, sem, out_sem,
):
    group = lax.axis_index("star")
    depth = MAPS * BLK // CHUNKS
    small = [
        pltpu.make_async_copy(a, b, sem.at[CHUNKS + i])
        for i, (a, b) in enumerate(
            [(seeds_hbm, seeds), (counts_hbm, counts_ref), (cells_hbm, cells_ref), (bands_hbm, bands_ref), (table_hbm, table)]
        )
    ]
    for copy in small:
        copy.start()
    loads = []
    for c in range(CHUNKS):
        rows = pl.ds(c * depth, depth)
        load = pltpu.make_async_copy(maps_hbm.at[rows], maps.at[rows], sem.at[c])
        load.start()
        loads.append(load)
    small[0].wait()
    cb, sb = seeds[0, 0], seeds[0, 1]
    for a in range(16):
        ca, sa = seeds[1, 0, a : a + 1, :], seeds[1, 1, a : a + 1, :]
        tables[0, a * 32 : a * 32 + 32, :] = (ca * cb - sa * sb).astype(BF)
        tables[1, a * 32 : a * 32 + 32, :] = (ca * sb + sa * cb).astype(BF)
    for copy in small[1:]:
        copy.wait()
    counts = [counts_ref[g] for g in range(GROUPS)]
    place = iota((64, MAPS), 0)
    slots = jnp.where((place & 7) < MINE, assigned(place >> 3, place & 7, counts), -1)
    cell = jnp.full((64, MAPS), -1, jnp.int32)
    for g in range(GROUPS):
        for j in range(SLOT):
            cell = jnp.where(slots == g * SLOT + j, cells_ref[g, j], cell)
    hot = jnp.where(iota((64, MAPS), 1) == cell, 1.0, 0.0)
    hot_ref[...] = hot
    coef_ref[...] = dot(hot.astype(BF), table[...]).astype(BF)
    turns = []
    for t in range(MINE):
        slot = assigned(group, jnp.int32(t), counts)
        band = bands_ref[slot // SLOT, slot % SLOT]
        meta_ref[t] = slot
        meta_ref[MINE + t] = band
        turns.append(pick(TURNS, band))
    for k in range(1, 4):
        other = (group + 2 * k) & 7
        for t in range(1, MINE):
            slot = assigned(other, jnp.int32(t), counts)
            meta_ref[2 * MINE + 3 * (k - 1) + t - 1] = jnp.where((slot // SLOT) >> 1 == group >> 1, slot, -1)
    mine = jnp.where(iota((128, 64), 1) == group * 8 + (iota((128, 64), 0) >> 5), 1.0, 0.0)
    rows = dot(mine.astype(BF), coef_ref[...]).astype(BF)
    same = same_pixel((128, depth))
    k = iota((MAPS, depth), 0)
    for c in range(CHUNKS):
        each = jnp.where(k == c * (MAPS // CHUNKS) + (iota((MAPS, depth), 1) >> 5), 1.0, 0.0).astype(BF)
        wide = dot(rows, each)
        spread[:, c * depth : (c + 1) * depth] = jnp.where(same, wide, 0.0).astype(BF)
    for c in range(CHUNKS):
        loads[c].wait()
        part = dot(spread[:, c * depth : (c + 1) * depth], maps[c * depth : (c + 1) * depth, :])
        path[...] = part if c == 0 else path[...] + part
    first = lax.axis_index("row") * BLK
    for h in range(BLK // 16):
        inside = aperture_mask(first + h * 16, 16)
        for t in range(MINE):
            at = slice(t * BLK + h * 16, t * BLK + h * 16 + 16)
            x = path[at, :] * turns[t]
            f = x - jnp.round(x)
            frac_ref[at, :] = f
            c, s = cos_sin_turns(f)
            for part, value in enumerate((c, s)):
                value = jnp.where(inside, value, 0.0)
                field[slice(at.start + part * 128, at.stop + part * 128), :] = value.astype(BF)
                field[slice(at.start + part * 128 + 256, at.stop + part * 128 + 256), :] = alternate(value).astype(BF)
    stores = [pltpu.make_async_copy(frac_ref, frac_hbm, out_sem.at[4])]
    stores[0].start()
    for m in range(2):
        by_cos, by_sin = table_times(tables, field, slice(m * 256, m * 256 + 256))
        for half in range(2):
            at = slice(half * 512 + m * 256, half * 512 + m * 256 + 256)
            re, im = slice(half * 256, half * 256 + 128), slice(half * 256 + 128, half * 256 + 256)
            sent_ref[at, :128] = (by_cos[:, re] - by_sin[:, im]).astype(BF)
            sent_ref[at, 128:] = (by_sin[:, re] + by_cos[:, im]).astype(BF)
            stores.append(pltpu.make_async_copy(sent_ref.at[at], sent_hbm.at[at], out_sem.at[2 * m + half]))
            stores[-1].start()
    for store in stores:
        store.wait()


def pupil(counts, cells, bands, table, seeds, maps):
    return pl.pallas_call(
        pupil_kernel,
        name="pupil",
        out_shape=[
            pltpu.HBM((N, 256), BF),
            pltpu.HBM((MINE * BLK, N), F32),
            jax.ShapeDtypeStruct((2, N // 2, N), BF),
            jax.ShapeDtypeStruct((64, MAPS), F32),
            jax.ShapeDtypeStruct((64, MAPS), BF),
            jax.ShapeDtypeStruct((2 * MINE + 9,), jnp.int32),
        ],
        in_specs=[HBM_SPEC] * 6,
        out_specs=[HBM_SPEC] * 2 + [VMEM_SPEC] * 3 + [SMEM_SPEC],
        scratch_shapes=[
            pltpu.SMEM((GROUPS,), jnp.int32),
            pltpu.SMEM((GROUPS, SLOT), jnp.int32),
            pltpu.SMEM((GROUPS, SLOT), jnp.int32),
            pltpu.VMEM((64, MAPS), BF),
            pltpu.VMEM((2, 2, 32, N), F32),
            pltpu.VMEM((MAPS * BLK, N), BF),
            pltpu.VMEM((MINE * BLK, MAPS * BLK), BF),
            pltpu.VMEM((512, N), BF),
            pltpu.VMEM((MINE * BLK, N), F32),
            pltpu.VMEM((N, 256), BF),
            pltpu.VMEM((MINE * BLK, N), F32),
            pltpu.SemaphoreType.DMA((CHUNKS + 5,)),
            pltpu.SemaphoreType.DMA((5,)),
        ],
        compiler_params=params(20),
    )(*in_hbm(counts, cells, bands, table, seeds, maps))


def gather_blocks(got_ref, out_ref):
    lane = iota((BLK, 128), 1)
    low = lane < 64
    even = (lane & 63) < 32
    for part in range(2):
        for quad in range(8):
            x = [
                got_ref[(4 * quad + i) * BLK : (4 * quad + i + 1) * BLK, part * 128 : part * 128 + 128].astype(F32)
                for i in range(4)
            ]
            y = [None] * 4
            for i in range(2):
                y[i] = jnp.where(low, x[i], pltpu.roll(x[i + 2], 64, 1))
                y[i + 2] = jnp.where(low, pltpu.roll(x[i], 64, 1), x[i + 2])
            z = [None] * 4
            for i in (0, 2):
                z[i] = jnp.where(even, y[i], pltpu.roll(y[i + 1], 32, 1))
                z[i + 1] = jnp.where(even, pltpu.roll(y[i], 96, 1), y[i + 1])
            for s in range(4):
                at = part * 128 + s * BLK
                out_ref[at : at + BLK, quad * 128 : quad * 128 + 128] = z[s].astype(BF)


def pack_kernel(meta_ref, own_hbm, twin_hbm, one_hbm, two_hbm, three_hbm, held, in_sem, out_sem):
    group = lax.axis_index("star")
    sent = (one_hbm, two_hbm, three_hbm)
    for i in range(9):
        slot = meta_ref[2 * MINE + i]
        place = jnp.maximum(slot, 0) % SLOT
        mine = slot // SLOT == group

        @pl.when((slot >= 0) & mine)
        def _():
            pltpu.make_async_copy(own_hbm.at[place], held.at[i], in_sem.at[i]).start()

        @pl.when((slot >= 0) & jnp.logical_not(mine))
        def _():
            pltpu.make_async_copy(twin_hbm.at[place], held.at[i], in_sem.at[i]).start()

    for i in range(9):

        @pl.when(meta_ref[2 * MINE + i] >= 0)
        def _():
            pltpu.make_async_copy(own_hbm.at[0], held.at[i], in_sem.at[i]).wait()
            pltpu.make_async_copy(held.at[i], sent[i // 3].at[i % 3], out_sem.at[i]).start()

    for i in range(9):

        @pl.when(meta_ref[2 * MINE + i] >= 0)
        def _():
            pltpu.make_async_copy(held.at[i], sent[i // 3].at[i % 3], out_sem.at[i]).wait()


def pack(meta, own, twin):
    return pl.pallas_call(
        pack_kernel,
        name="pack",
        out_shape=[pltpu.HBM((3, BLK, N), BF)] * 3,
        in_specs=[SMEM_SPEC, HBM_SPEC, ANY_SPEC],
        out_specs=[HBM_SPEC] * 3,
        scratch_shapes=[
            pltpu.VMEM((9, BLK, N), BF),
            pltpu.SemaphoreType.DMA((9,)),
            pltpu.SemaphoreType.DMA((9,)),
        ],
        compiler_params=params(4),
    )(meta, *in_hbm(own), twin)


def focal_kernel(
    meta_ref, got_ref, tables, own_hbm, twin_hbm, one_hbm, two_hbm, three_hbm, sent_ref, cot, field, grad, sem
):
    group = lax.axis_index("star")
    for t in range(MINE):
        slot = meta_ref[t]
        owner = slot // SLOT
        place = slot % SLOT
        hop = ((group >> 1) - (owner >> 1)) & 3

        @pl.when((hop == 0) & (owner == group))
        def _():
            pltpu.make_async_copy(own_hbm.at[place], cot.at[t], sem.at[t]).start()

        @pl.when((hop == 0) & (owner != group))
        def _():
            pltpu.make_async_copy(twin_hbm.at[place], cot.at[t], sem.at[t]).start()

        for k, got in ((1, one_hbm), (2, two_hbm), (3, three_hbm)):

            @pl.when(hop == k)
            def _():
                pltpu.make_async_copy(got.at[max(t - 1, 0)], cot.at[t], sem.at[t]).start()

    gather_blocks(got_ref, field)
    for n in range(4):
        at = slice(n * 256, n * 256 + 256)
        by_cos = times_table(field, tables.at[0], at)
        by_sin = times_table(field, tables.at[1], at)
        if n == 0:
            for t in range(MINE):
                pltpu.make_async_copy(own_hbm.at[t], cot.at[t], sem.at[t]).wait()
        weight = cot[:, :, at].reshape(128, 256).astype(F32) * (2.0 / N)
        for part, value in enumerate((by_cos[:128] - by_sin[128:], by_sin[:128] + by_cos[128:])):
            value = weight * value
            grad[slice(part * 128, part * 128 + 128), at] = value.astype(BF)
            grad[slice(part * 128 + 256, part * 128 + 384), at] = alternate(value).astype(BF)
    for m in range(2):
        by_cos, by_sin = table_times(tables, grad, slice(m * 256, m * 256 + 256))
        for half in range(2):
            at = slice(half * 512 + m * 256, half * 512 + m * 256 + 256)
            re, im = slice(half * 256, half * 256 + 128), slice(half * 256 + 128, half * 256 + 256)
            sent_ref[at, :128] = ((by_cos[:, re] + by_sin[:, im]) * (1.0 / N)).astype(BF)
            sent_ref[at, 128:] = ((by_cos[:, im] - by_sin[:, re]) * (1.0 / N)).astype(BF)


def focal(meta, got, tables, own, twin, moved):
    return pl.pallas_call(
        focal_kernel,
        name="focal",
        out_shape=jax.ShapeDtypeStruct((N, 256), BF),
        in_specs=[SMEM_SPEC, VMEM_SPEC, VMEM_SPEC] + [HBM_SPEC] * 5,
        out_specs=VMEM_SPEC,
        scratch_shapes=[
            pltpu.VMEM((MINE, BLK, N), BF),
            pltpu.VMEM((256, N), BF),
            pltpu.VMEM((512, N), BF),
            pltpu.SemaphoreType.DMA((MINE,)),
        ],
        compiler_params=params(16),
    )(meta, got, tables, *in_hbm(own, twin, *moved))


def back_kernel(meta_ref, got_ref, tables, frac_hbm, path_grad_ref, frac_ref, field, in_sem):
    load = pltpu.make_async_copy(frac_hbm, frac_ref, in_sem)
    load.start()
    gather_blocks(got_ref, field)
    waves = [pick(WAVES, meta_ref[MINE + t]) for t in range(MINE)]
    inside = aperture_mask(lax.axis_index("row") * BLK, BLK)
    for n in range(4):
        at = slice(n * 256, n * 256 + 256)
        by_cos = times_table(field, tables.at[0], at)
        by_sin = times_table(field, tables.at[1], at)
        real = by_cos[:128] + by_sin[128:]
        imag = by_cos[128:] - by_sin[:128]
        if n == 0:
            load.wait()
        for t in range(MINE):
            rows = slice(t * BLK, t * BLK + BLK)
            c, s = cos_sin_turns(frac_ref[rows, at])
            grad = waves[t] * (c * imag[rows] - s * real[rows])
            path_grad_ref[rows, at] = jnp.where(inside[:, at], grad, 0.0).astype(BF)


def back(meta, got, tables, frac):
    return pl.pallas_call(
        back_kernel,
        name="back",
        out_shape=jax.ShapeDtypeStruct((MINE * BLK, N), BF),
        in_specs=[SMEM_SPEC, VMEM_SPEC, VMEM_SPEC, HBM_SPEC],
        out_specs=VMEM_SPEC,
        scratch_shapes=[
            pltpu.VMEM((MINE * BLK, N), F32),
            pltpu.VMEM((256, N), BF),
            pltpu.SemaphoreType.DMA,
        ],
        compiler_params=params(16),
    )(meta, got, tables, *in_hbm(frac))


def score_kernel(path_grad_ref, maps_ref, score_ref):
    parts = []
    same = same_pixel((256, 128))
    for c in range(8):
        some = dot(maps_ref[c * 256 : (c + 1) * 256, :], path_grad_ref[...], NT)
        kept = jnp.where(same, some, 0.0)
        for k in range(8):
            parts.append(jnp.sum(kept[k * BLK : (k + 1) * BLK], axis=0, keepdims=True))
    by_lane = jnp.concatenate(parts, axis=0)
    pick_star = jnp.where((iota((8, 128), 1) >> 5) == iota((8, 128), 0), 1.0, 0.0)
    scores = dot(pick_star, by_lane, NT, lax.Precision.HIGHEST)
    for j in range(2):
        pair = jnp.concatenate([scores[2 * j : 2 * j + 1], scores[2 * j + 1 : 2 * j + 2]], axis=1)
        score_ref[:, j, :] = jnp.broadcast_to(pair, (32, 128))


def score_of(path_grad, maps):
    return pl.pallas_call(
        score_kernel,
        name="score",
        out_shape=jax.ShapeDtypeStruct((32, 2, 128), F32),
        in_specs=[VMEM_SPEC, VMEM_SPEC],
        out_specs=VMEM_SPEC,
        compiler_params=params(16),
    )(path_grad, maps)


def total_kernel(coef_ref, hot_ref, score_ref, *refs):
    blocks = refs[: 2 * MINE]
    map_grad_hbm, coef_grad_ref, path_grad, map_grad, out_sem = refs[2 * MINE :]
    group = lax.axis_index("star")
    for i, block in enumerate(blocks):
        h = (group ^ (i // MINE)) - 2 * (i % MINE) & (GROUPS - 1)
        path_grad[pl.ds(pl.multiple_of(h * 128, 128), 128), :] = block[...]
    share = MAPS // GROUPS
    mine = jnp.where(iota((share * BLK, MAPS), 1) == group * share + (iota((share * BLK, MAPS), 0) >> 5), 1.0, 0.0)
    rows = dot(mine.astype(BF), coef_ref[...], NT).astype(BF)
    q = iota((64, N), 1) >> 5
    each = jnp.where(iota((64, N), 0) == ((q >> 2) << 3) + (q & 3), 1.0, 0.0).astype(BF)
    wide = dot(rows, each)
    spread = jnp.where(same_pixel(wide.shape), wide, 0.0).astype(BF)
    stores = []
    for m in range(2):
        at = slice(m * 128, m * 128 + 128)
        map_grad[at, :] = dot(spread[at], path_grad[...])
        store = pltpu.make_async_copy(map_grad.at[at], map_grad_hbm.at[at], out_sem.at[m])
        store.start()
        stores.append(store)
    grads = []
    for half in range(2):
        grad = jnp.zeros((64, 128), F32)
        for j in range(2):
            place = iota((GROUPS, 64), 0) * 8 + 2 * j + half
            rows = dot(jnp.where(iota((GROUPS, 64), 1) == place, 1.0, 0.0), hot_ref[...])
            grad = grad + dot(rows, score_ref[:, j, :], TN, lax.Precision.HIGHEST)
        grads.append(grad[:, half * MAPS : half * MAPS + MAPS])
    coef_grad_ref[...] = (grads[0] + grads[1]) * (1.0 / (8 * N))
    for store in stores:
        store.wait()


def total(coef, hot, scores, blocks):
    rows = MAPS // GROUPS * BLK
    return pl.pallas_call(
        total_kernel,
        name="total",
        out_shape=[pltpu.HBM((rows, N), F32), jax.ShapeDtypeStruct((64, MAPS), F32)],
        in_specs=[VMEM_SPEC] * 11,
        out_specs=[HBM_SPEC, VMEM_SPEC],
        scratch_shapes=[
            pltpu.VMEM((N, N), BF),
            pltpu.VMEM((rows, N), F32),
            pltpu.SemaphoreType.DMA((2,)),
        ],
        compiler_params=params(16),
    )(coef, hot, scores, *blocks)


def swap_cores(x):
    return lax.ppermute(x, "star", [(g, g ^ 1) for g in range(GROUPS)])


def along_x(x, k):
    return lax.ppermute(x, "star", [(g, (g + 2 * k) % GROUPS) for g in range(GROUPS)])


def per_device(feature_maps, coef_table, star_counts, star_cells, star_bands, psf_cotangent):
    maps = feature_maps.reshape(MAPS * BLK, N)
    twin = swap_cores(psf_cotangent)
    sent, frac, tables, hot, coef, meta = pupil(
        star_counts, star_cells, star_bands, coef_table, jnp.asarray(table_seeds()), maps
    )
    sent, *packed = lax.optimization_barrier((sent, *pack(meta, psf_cotangent, twin)))
    moved = [along_x(packed[k - 1], k) for k in (1, 2, 3)]
    got = lax.all_to_all(sent.reshape(32, BLK, 256), "row", 0, 0, tiled=True).reshape(N, 256)
    sent = focal(meta, got, tables, psf_cotangent, twin, moved)
    got = lax.all_to_all(sent.reshape(32, BLK, 256), "row", 0, 0, tiled=True).reshape(N, 256)
    path_grad = back(meta, got, tables, frac)
    blocks = [path_grad] + [along_x(path_grad, k) for k in (1, 2, 3)]
    score = lax.all_to_all(score_of(path_grad, maps), "row", 0, 0, tiled=True)
    score, *blocks = lax.optimization_barrier((score, *blocks))
    blocks = blocks + [swap_cores(block) for block in blocks]
    score = jnp.broadcast_to(jnp.sum(score, 0)[None], (GROUPS, 2, 128))
    score = lax.all_to_all(score, "star", 0, 0, tiled=True)
    map_grad, coef_grad = total(coef, hot, score, blocks)
    return map_grad.reshape(MAPS // GROUPS, BLK, N), coef_grad


def solution(mesh):
    placed = (P(None, "row", None), P(), P(), P(), P(), P("star", "row", None))
    return jax.shard_map(
        per_device,
        mesh=mesh,
        in_specs=placed,
        out_specs=(P("star", "row", None), P()),
        check_vma=False,
    )
```

```python
import jax
import jax.numpy as jnp
import numpy as np
from jax import lax
from jax.experimental import pallas as pl
from jax.experimental.pallas import tpu as pltpu
from jax.sharding import PartitionSpec as P

BF = jnp.bfloat16
F32 = jnp.float32
N = 1024
MAPS = 64
BLK = 32
GROUPS = 8
SLOT = 12
TOTAL = 32
MINE = 4
WAVES = [float(np.float32(2.0 * np.pi) / np.float32(0.55 + 0.35 * b / 7)) for b in range(8)]
TURNS = [float(1.0 / (0.55 + 0.35 * b / 7)) for b in range(8)]
VMEM_SPEC = pl.BlockSpec(memory_space=pltpu.VMEM)
SMEM_SPEC = pl.BlockSpec(memory_space=pltpu.SMEM)
HBM_SPEC = pl.BlockSpec(memory_space=pltpu.HBM)
ANY_SPEC = pl.BlockSpec(memory_space=pl.ANY)
NN = (((1,), (0,)), ((), ()))
NT = (((1,), (1,)), ((), ()))
TN = (((0,), (0,)), ((), ()))


def dot(a, b, dims=NN, precision=None):
    return lax.dot_general(a, b, dims, precision=precision, preferred_element_type=F32)


def iota(shape, axis):
    return lax.broadcasted_iota(jnp.int32, shape, axis)


def in_hbm(*arrays):
    return [pltpu.with_memory_space_constraint(a, pltpu.HBM) for a in arrays]


def params(mib):
    return pltpu.CompilerParams(vmem_limit_bytes=mib << 20)


def table_seeds():
    b = np.arange(N, dtype=np.int64)
    low = (np.arange(32)[:, None] * b[None, :]) % N
    high = (32 * (np.arange(32) % 16)[:, None] * b[None, :]) % N
    both = np.stack([low, high]) * (2.0 * np.pi / N)
    return np.stack([np.cos(both), -np.sin(both)], 1).astype(np.float32)


def fit_polynomials():
    x = 0.125 * (1.0 + np.cos(np.pi * (np.arange(4000) + 0.5) / 4000))
    f = np.sqrt(x)
    cheb = np.polynomial.chebyshev.Chebyshev
    poly = np.polynomial.polynomial.Polynomial
    c = cheb.fit(x, np.cos(2 * np.pi * f), 7, domain=[0, 0.25]).convert(kind=poly)
    s = cheb.fit(x, np.sin(2 * np.pi * f) / f, 6, domain=[0, 0.25]).convert(kind=poly)
    return [float(v) for v in c.coef], [float(v) for v in s.coef]


COS_POLY, SIN_POLY = fit_polynomials()


def cos_sin_turns(f):
    x = f * f
    c = jnp.full_like(f, COS_POLY[-1])
    s = jnp.full_like(f, SIN_POLY[-1])
    for a in COS_POLY[-2::-1]:
        c = c * x + a
    for a in SIN_POLY[-2::-1]:
        s = s * x + a
    return c, s * f


def assigned(h, t, counts):
    before, count, free = jnp.zeros_like(h), jnp.zeros_like(h), jnp.int32(0)
    for g in range(GROUPS):
        before = jnp.where(h == g, free, before)
        count = jnp.where(h == g, counts[g], count)
        free = free + jnp.maximum(MINE - counts[g], 0)
    e = before + t - count
    slot, first = jnp.zeros_like(h), jnp.int32(0)
    for g in range(GROUPS):
        after = first + jnp.maximum(counts[g] - MINE, 0)
        slot = jnp.where((e >= first) & (e < after), g * SLOT + MINE + e - first, slot)
        first = after
    return jnp.where(t < count, h * SLOT + t, slot)


def pick(values, index):
    chosen = jnp.float32(values[0])
    for k in range(1, len(values)):
        chosen = jnp.where(index == k, jnp.float32(values[k]), chosen)
    return chosen


def aperture_mask(first_row, rows):
    centre = 0.5 * (N - 1)
    y = (first_row + iota((rows, N), 0)).astype(F32) - centre
    x = iota((rows, N), 1).astype(F32) - centre
    return y * y + x * x <= 0.25 * N * N


def alternate(x):
    return x * jnp.where((iota((1, x.shape[1]), 1) & 1) == 0, 1.0, -1.0)


def same_pixel(shape):
    return ((iota(shape, 0) ^ iota(shape, 1)) & (BLK - 1)) == 0


def times_table(field, table, at):
    upper = dot(field[:, : N // 2], table[:, at])
    lower = dot(field[:, N // 2 :], table[:, at])
    return upper + alternate(lower)


def table_times(tables, both, at):
    return dot(tables[0, at, :], both[...], NT), dot(tables[1, at, :], both[...], NT)


CHUNKS = 2


def pupil_kernel(
    counts_hbm, cells_hbm, bands_hbm, table_hbm, seeds_hbm, maps_hbm,
    sent_hbm, frac_hbm, tables, hot_ref, coef_ref, meta_ref,
    counts_ref, cells_ref, bands_ref, table, seeds, maps, spread, field, path, sent_ref, frac_ref, sem, out_sem,
):
    group = lax.axis_index("star")
    depth = MAPS * BLK // CHUNKS
    small = [
        pltpu.make_async_copy(a, b, sem.at[CHUNKS + i])
        for i, (a, b) in enumerate(
            [(seeds_hbm, seeds), (counts_hbm, counts_ref), (cells_hbm, cells_ref), (bands_hbm, bands_ref), (table_hbm, table)]
        )
    ]
    for copy in small:
        copy.start()
    loads = []
    for c in range(CHUNKS):
        rows = pl.ds(c * depth, depth)
        load = pltpu.make_async_copy(maps_hbm.at[rows], maps.at[rows], sem.at[c])
        load.start()
        loads.append(load)
    small[0].wait()
    cb, sb = seeds[0, 0], seeds[0, 1]
    for a in range(16):
        ca, sa = seeds[1, 0, a : a + 1, :], seeds[1, 1, a : a + 1, :]
        tables[0, a * 32 : a * 32 + 32, :] = (ca * cb - sa * sb).astype(BF)
        tables[1, a * 32 : a * 32 + 32, :] = (ca * sb + sa * cb).astype(BF)
    for copy in small[1:]:
        copy.wait()
    counts = [counts_ref[g] for g in range(GROUPS)]
    place = iota((64, MAPS), 0)
    slots = jnp.where((place & 7) < MINE, assigned(place >> 3, place & 7, counts), -1)
    cell = jnp.full((64, MAPS), -1, jnp.int32)
    for g in range(GROUPS):
        for j in range(SLOT):
            cell = jnp.where(slots == g * SLOT + j, cells_ref[g, j], cell)
    hot = jnp.where(iota((64, MAPS), 1) == cell, 1.0, 0.0)
    hot_ref[...] = hot
    coef_ref[...] = dot(hot.astype(BF), table[...]).astype(BF)
    turns = []
    for t in range(MINE):
        slot = assigned(group, jnp.int32(t), counts)
        band = bands_ref[slot // SLOT, slot % SLOT]
        meta_ref[t] = slot
        meta_ref[MINE + t] = band
        turns.append(pick(TURNS, band))
    for k in range(1, 4):
        other = (group + 2 * k) & 7
        for t in range(1, MINE):
            slot = assigned(other, jnp.int32(t), counts)
            meta_ref[2 * MINE + 3 * (k - 1) + t - 1] = jnp.where((slot // SLOT) >> 1 == group >> 1, slot, -1)
    mine = jnp.where(iota((128, 64), 1) == group * 8 + (iota((128, 64), 0) >> 5), 1.0, 0.0)
    rows = dot(mine.astype(BF), coef_ref[...]).astype(BF)
    same = same_pixel((128, depth))
    k = iota((MAPS, depth), 0)
    for c in range(CHUNKS):
        each = jnp.where(k == c * (MAPS // CHUNKS) + (iota((MAPS, depth), 1) >> 5), 1.0, 0.0).astype(BF)
        wide = dot(rows, each)
        spread[:, c * depth : (c + 1) * depth] = jnp.where(same, wide, 0.0).astype(BF)
    for c in range(CHUNKS):
        loads[c].wait()
        part = dot(spread[:, c * depth : (c + 1) * depth], maps[c * depth : (c + 1) * depth, :])
        path[...] = part if c == 0 else path[...] + part
    first = lax.axis_index("row") * BLK
    for h in range(BLK // 16):
        inside = aperture_mask(first + h * 16, 16)
        for t in range(MINE):
            at = slice(t * BLK + h * 16, t * BLK + h * 16 + 16)
            x = path[at, :] * turns[t]
            f = x - jnp.round(x)
            frac_ref[at, :] = f
            c, s = cos_sin_turns(f)
            for part, value in enumerate((c, s)):
                value = jnp.where(inside, value, 0.0)
                field[slice(at.start + part * 128, at.stop + part * 128), :] = value.astype(BF)
                field[slice(at.start + part * 128 + 256, at.stop + part * 128 + 256), :] = alternate(value).astype(BF)
    stores = [pltpu.make_async_copy(frac_ref, frac_hbm, out_sem.at[4])]
    stores[0].start()
    for m in range(2):
        by_cos, by_sin = table_times(tables, field, slice(m * 256, m * 256 + 256))
        for half in range(2):
            at = slice(half * 512 + m * 256, half * 512 + m * 256 + 256)
            re, im = slice(half * 256, half * 256 + 128), slice(half * 256 + 128, half * 256 + 256)
            sent_ref[at, :128] = (by_cos[:, re] - by_sin[:, im]).astype(BF)
            sent_ref[at, 128:] = (by_sin[:, re] + by_cos[:, im]).astype(BF)
            stores.append(pltpu.make_async_copy(sent_ref.at[at], sent_hbm.at[at], out_sem.at[2 * m + half]))
            stores[-1].start()
    for store in stores:
        store.wait()


def pupil(counts, cells, bands, table, seeds, maps):
    return pl.pallas_call(
        pupil_kernel,
        name="pupil",
        out_shape=[
            pltpu.HBM((N, 256), BF),
            pltpu.HBM((MINE * BLK, N), F32),
            jax.ShapeDtypeStruct((2, N // 2, N), BF),
            jax.ShapeDtypeStruct((64, MAPS), F32),
            jax.ShapeDtypeStruct((64, MAPS), BF),
            jax.ShapeDtypeStruct((2 * MINE + 9,), jnp.int32),
        ],
        in_specs=[HBM_SPEC] * 6,
        out_specs=[HBM_SPEC] * 2 + [VMEM_SPEC] * 3 + [SMEM_SPEC],
        scratch_shapes=[
            pltpu.SMEM((GROUPS,), jnp.int32),
            pltpu.SMEM((GROUPS, SLOT), jnp.int32),
            pltpu.SMEM((GROUPS, SLOT), jnp.int32),
            pltpu.VMEM((64, MAPS), BF),
            pltpu.VMEM((2, 2, 32, N), F32),
            pltpu.VMEM((MAPS * BLK, N), BF),
            pltpu.VMEM((MINE * BLK, MAPS * BLK), BF),
            pltpu.VMEM((512, N), BF),
            pltpu.VMEM((MINE * BLK, N), F32),
            pltpu.VMEM((N, 256), BF),
            pltpu.VMEM((MINE * BLK, N), F32),
            pltpu.SemaphoreType.DMA((CHUNKS + 5,)),
            pltpu.SemaphoreType.DMA((5,)),
        ],
        compiler_params=params(20),
    )(*in_hbm(counts, cells, bands, table, seeds, maps))


def gather_blocks(got_ref, out_ref):
    lane = iota((BLK, 128), 1)
    low = lane < 64
    even = (lane & 63) < 32
    for part in range(2):
        for quad in range(8):
            x = [
                got_ref[(4 * quad + i) * BLK : (4 * quad + i + 1) * BLK, part * 128 : part * 128 + 128].astype(F32)
                for i in range(4)
            ]
            y = [None] * 4
            for i in range(2):
                y[i] = jnp.where(low, x[i], pltpu.roll(x[i + 2], 64, 1))
                y[i + 2] = jnp.where(low, pltpu.roll(x[i], 64, 1), x[i + 2])
            z = [None] * 4
            for i in (0, 2):
                z[i] = jnp.where(even, y[i], pltpu.roll(y[i + 1], 32, 1))
                z[i + 1] = jnp.where(even, pltpu.roll(y[i], 96, 1), y[i + 1])
            for s in range(4):
                at = part * 128 + s * BLK
                out_ref[at : at + BLK, quad * 128 : quad * 128 + 128] = z[s].astype(BF)


def pack_kernel(meta_ref, own_hbm, twin_hbm, one_hbm, two_hbm, three_hbm, held, in_sem, out_sem):
    group = lax.axis_index("star")
    sent = (one_hbm, two_hbm, three_hbm)
    for i in range(9):
        slot = meta_ref[2 * MINE + i]
        place = jnp.maximum(slot, 0) % SLOT
        mine = slot // SLOT == group

        @pl.when((slot >= 0) & mine)
        def _():
            pltpu.make_async_copy(own_hbm.at[place], held.at[i], in_sem.at[i]).start()

        @pl.when((slot >= 0) & jnp.logical_not(mine))
        def _():
            pltpu.make_async_copy(twin_hbm.at[place], held.at[i], in_sem.at[i]).start()

    for i in range(9):

        @pl.when(meta_ref[2 * MINE + i] >= 0)
        def _():
            pltpu.make_async_copy(own_hbm.at[0], held.at[i], in_sem.at[i]).wait()
            pltpu.make_async_copy(held.at[i], sent[i // 3].at[i % 3], out_sem.at[i]).start()

    for i in range(9):

        @pl.when(meta_ref[2 * MINE + i] >= 0)
        def _():
            pltpu.make_async_copy(held.at[i], sent[i // 3].at[i % 3], out_sem.at[i]).wait()


def pack(meta, own, twin):
    return pl.pallas_call(
        pack_kernel,
        name="pack",
        out_shape=[pltpu.HBM((3, BLK, N), BF)] * 3,
        in_specs=[SMEM_SPEC, HBM_SPEC, ANY_SPEC],
        out_specs=[HBM_SPEC] * 3,
        scratch_shapes=[
            pltpu.VMEM((9, BLK, N), BF),
            pltpu.SemaphoreType.DMA((9,)),
            pltpu.SemaphoreType.DMA((9,)),
        ],
        compiler_params=params(4),
    )(meta, *in_hbm(own), twin)


def focal_kernel(
    meta_ref, got_ref, tables, own_hbm, twin_hbm, one_hbm, two_hbm, three_hbm, sent_ref, cot, field, grad, sem
):
    group = lax.axis_index("star")
    for t in range(MINE):
        slot = meta_ref[t]
        owner = slot // SLOT
        place = slot % SLOT
        hop = ((group >> 1) - (owner >> 1)) & 3

        @pl.when((hop == 0) & (owner == group))
        def _():
            pltpu.make_async_copy(own_hbm.at[place], cot.at[t], sem.at[t]).start()

        @pl.when((hop == 0) & (owner != group))
        def _():
            pltpu.make_async_copy(twin_hbm.at[place], cot.at[t], sem.at[t]).start()

        for k, got in ((1, one_hbm), (2, two_hbm), (3, three_hbm)):

            @pl.when(hop == k)
            def _():
                pltpu.make_async_copy(got.at[max(t - 1, 0)], cot.at[t], sem.at[t]).start()

    gather_blocks(got_ref, field)
    for n in range(4):
        at = slice(n * 256, n * 256 + 256)
        by_cos = times_table(field, tables.at[0], at)
        by_sin = times_table(field, tables.at[1], at)
        if n == 0:
            for t in range(MINE):
                pltpu.make_async_copy(own_hbm.at[t], cot.at[t], sem.at[t]).wait()
        weight = cot[:, :, at].reshape(128, 256).astype(F32) * (2.0 / N)
        for part, value in enumerate((by_cos[:128] - by_sin[128:], by_sin[:128] + by_cos[128:])):
            value = weight * value
            grad[slice(part * 128, part * 128 + 128), at] = value.astype(BF)
            grad[slice(part * 128 + 256, part * 128 + 384), at] = alternate(value).astype(BF)
    for m in range(2):
        by_cos, by_sin = table_times(tables, grad, slice(m * 256, m * 256 + 256))
        for half in range(2):
            at = slice(half * 512 + m * 256, half * 512 + m * 256 + 256)
            re, im = slice(half * 256, half * 256 + 128), slice(half * 256 + 128, half * 256 + 256)
            sent_ref[at, :128] = ((by_cos[:, re] + by_sin[:, im]) * (1.0 / N)).astype(BF)
            sent_ref[at, 128:] = ((by_cos[:, im] - by_sin[:, re]) * (1.0 / N)).astype(BF)


def focal(meta, got, tables, own, twin, moved):
    return pl.pallas_call(
        focal_kernel,
        name="focal",
        out_shape=jax.ShapeDtypeStruct((N, 256), BF),
        in_specs=[SMEM_SPEC, VMEM_SPEC, VMEM_SPEC] + [HBM_SPEC] * 5,
        out_specs=VMEM_SPEC,
        scratch_shapes=[
            pltpu.VMEM((MINE, BLK, N), BF),
            pltpu.VMEM((256, N), BF),
            pltpu.VMEM((512, N), BF),
            pltpu.SemaphoreType.DMA((MINE,)),
        ],
        compiler_params=params(16),
    )(meta, got, tables, *in_hbm(own, twin, *moved))


def back_kernel(meta_ref, got_ref, tables, frac_hbm, path_grad_ref, frac_ref, field, in_sem):
    load = pltpu.make_async_copy(frac_hbm, frac_ref, in_sem)
    load.start()
    gather_blocks(got_ref, field)
    waves = [pick(WAVES, meta_ref[MINE + t]) for t in range(MINE)]
    inside = aperture_mask(lax.axis_index("row") * BLK, BLK)
    for n in range(4):
        at = slice(n * 256, n * 256 + 256)
        by_cos = times_table(field, tables.at[0], at)
        by_sin = times_table(field, tables.at[1], at)
        real = by_cos[:128] + by_sin[128:]
        imag = by_cos[128:] - by_sin[:128]
        if n == 0:
            load.wait()
        for t in range(MINE):
            rows = slice(t * BLK, t * BLK + BLK)
            c, s = cos_sin_turns(frac_ref[rows, at])
            grad = waves[t] * (c * imag[rows] - s * real[rows])
            path_grad_ref[rows, at] = jnp.where(inside[:, at], grad, 0.0).astype(BF)


def back(meta, got, tables, frac):
    return pl.pallas_call(
        back_kernel,
        name="back",
        out_shape=jax.ShapeDtypeStruct((MINE * BLK, N), BF),
        in_specs=[SMEM_SPEC, VMEM_SPEC, VMEM_SPEC, HBM_SPEC],
        out_specs=VMEM_SPEC,
        scratch_shapes=[
            pltpu.VMEM((MINE * BLK, N), F32),
            pltpu.VMEM((256, N), BF),
            pltpu.SemaphoreType.DMA,
        ],
        compiler_params=params(16),
    )(meta, got, tables, *in_hbm(frac))


def score_kernel(path_grad_ref, maps_ref, score_ref):
    parts = []
    same = same_pixel((256, 128))
    for c in range(8):
        some = dot(maps_ref[c * 256 : (c + 1) * 256, :], path_grad_ref[...], NT)
        kept = jnp.where(same, some, 0.0)
        for k in range(8):
            parts.append(jnp.sum(kept[k * BLK : (k + 1) * BLK], axis=0, keepdims=True))
    by_lane = jnp.concatenate(parts, axis=0)
    pick_star = jnp.where((iota((8, 128), 1) >> 5) == iota((8, 128), 0), 1.0, 0.0)
    scores = dot(pick_star, by_lane, NT, lax.Precision.HIGHEST)
    for j in range(2):
        pair = jnp.concatenate([scores[2 * j : 2 * j + 1], scores[2 * j + 1 : 2 * j + 2]], axis=1)
        score_ref[:, j, :] = jnp.broadcast_to(pair, (32, 128))


def score_of(path_grad, maps):
    return pl.pallas_call(
        score_kernel,
        name="score",
        out_shape=jax.ShapeDtypeStruct((32, 2, 128), F32),
        in_specs=[VMEM_SPEC, VMEM_SPEC],
        out_specs=VMEM_SPEC,
        compiler_params=params(16),
    )(path_grad, maps)


def total_kernel(coef_ref, hot_ref, score_ref, *refs):
    blocks = refs[: 2 * MINE]
    map_grad_hbm, coef_grad_ref, path_grad, map_grad, out_sem = refs[2 * MINE :]
    group = lax.axis_index("star")
    for i, block in enumerate(blocks):
        h = (group ^ (i // MINE)) - 2 * (i % MINE) & (GROUPS - 1)
        path_grad[pl.ds(pl.multiple_of(h * 128, 128), 128), :] = block[...]
    share = MAPS // GROUPS
    mine = jnp.where(iota((share * BLK, MAPS), 1) == group * share + (iota((share * BLK, MAPS), 0) >> 5), 1.0, 0.0)
    rows = dot(mine.astype(BF), coef_ref[...], NT).astype(BF)
    q = iota((64, N), 1) >> 5
    each = jnp.where(iota((64, N), 0) == ((q >> 2) << 3) + (q & 3), 1.0, 0.0).astype(BF)
    wide = dot(rows, each)
    spread = jnp.where(same_pixel(wide.shape), wide, 0.0).astype(BF)
    stores = []
    for m, at in enumerate((slice(0, 128), slice(128, 192), slice(192, 256))):
        map_grad[at, :] = dot(spread[at], path_grad[...])
        store = pltpu.make_async_copy(map_grad.at[at], map_grad_hbm.at[at], out_sem.at[m])
        store.start()
        stores.append(store)
    grads = []
    for half in range(2):
        grad = jnp.zeros((64, 128), F32)
        for j in range(2):
            place = iota((GROUPS, 64), 0) * 8 + 2 * j + half
            rows = dot(jnp.where(iota((GROUPS, 64), 1) == place, 1.0, 0.0), hot_ref[...])
            grad = grad + dot(rows, score_ref[:, j, :], TN, lax.Precision.HIGHEST)
        grads.append(grad[:, half * MAPS : half * MAPS + MAPS])
    coef_grad_ref[...] = (grads[0] + grads[1]) * (1.0 / (8 * N))
    for store in stores:
        store.wait()


def total(coef, hot, scores, blocks):
    rows = MAPS // GROUPS * BLK
    return pl.pallas_call(
        total_kernel,
        name="total",
        out_shape=[pltpu.HBM((rows, N), F32), jax.ShapeDtypeStruct((64, MAPS), F32)],
        in_specs=[VMEM_SPEC] * 11,
        out_specs=[HBM_SPEC, VMEM_SPEC],
        scratch_shapes=[
            pltpu.VMEM((N, N), BF),
            pltpu.VMEM((rows, N), F32),
            pltpu.SemaphoreType.DMA((3,)),
        ],
        compiler_params=params(16),
    )(coef, hot, scores, *blocks)


def swap_cores(x):
    return lax.ppermute(x, "star", [(g, g ^ 1) for g in range(GROUPS)])


def along_x(x, k):
    return lax.ppermute(x, "star", [(g, (g + 2 * k) % GROUPS) for g in range(GROUPS)])


def per_device(feature_maps, coef_table, star_counts, star_cells, star_bands, psf_cotangent):
    maps = feature_maps.reshape(MAPS * BLK, N)
    twin = swap_cores(psf_cotangent)
    sent, frac, tables, hot, coef, meta = pupil(
        star_counts, star_cells, star_bands, coef_table, jnp.asarray(table_seeds()), maps
    )
    sent, *packed = lax.optimization_barrier((sent, *pack(meta, psf_cotangent, twin)))
    moved = [along_x(packed[k - 1], k) for k in (1, 2, 3)]
    got = lax.all_to_all(sent.reshape(32, BLK, 256), "row", 0, 0, tiled=True).reshape(N, 256)
    sent = focal(meta, got, tables, psf_cotangent, twin, moved)
    got = lax.all_to_all(sent.reshape(32, BLK, 256), "row", 0, 0, tiled=True).reshape(N, 256)
    path_grad = back(meta, got, tables, frac)
    blocks = [path_grad] + [along_x(path_grad, k) for k in (1, 2, 3)]
    score = lax.all_to_all(score_of(path_grad, maps), "row", 0, 0, tiled=True)
    score, *blocks = lax.optimization_barrier((score, *blocks))
    blocks = blocks + [swap_cores(block) for block in blocks]
    score = jnp.broadcast_to(jnp.sum(score, 0)[None], (GROUPS, 2, 128))
    score = lax.all_to_all(score, "star", 0, 0, tiled=True)
    map_grad, coef_grad = total(coef, hot, score, blocks)
    return map_grad.reshape(MAPS // GROUPS, BLK, N), coef_grad


def solution(mesh):
    placed = (P(None, "row", None), P(), P(), P(), P(), P("star", "row", None))
    return jax.shard_map(
        per_device,
        mesh=mesh,
        in_specs=placed,
        out_specs=(P("star", "row", None), P()),
        check_vma=False,
    )
```
